32 devices in a mesh: graph: 8 (over z, x), batch: 4 (over y, core).
Axes of the slice: x: 2, y: 2, z: 4, core: 2. Of those that a mesh axis runs over, the one named last changes fastest.
Arguments:
- layer_input: bfloat16 [2048, 512], P('graph', 'batch'), may hold values from -6 to 6
- hidden_state: bfloat16 [2048, 512], P('graph', 'batch'), may hold values from -6 to 6
- hidden_grad: bfloat16 [2048, 512], P('graph', 'batch'), may hold values from -6 to 6
- gate_weight: bfloat16 [640, 128], replicated, may hold values from -0.25 to 0.25
- gate_bias: float32 [128], replicated, may hold values from -3 to 3
- candidate_weight: bfloat16 [640, 64], replicated, may hold values from -0.25 to 0.25
- candidate_bias: float32 [64], replicated, may hold values from -3 to 3
- forward_tiles: bfloat16 [16, 3, 128, 128], P('graph'), as said below
- forward_columns: int32 [16, 3], P('graph'), may hold values from 0 to 2
- reverse_tiles: bfloat16 [16, 3, 128, 128], P('graph'), as said below
- reverse_columns: int32 [16, 3], P('graph'), may hold values from 0 to 2
- send_rows: int32 [8, 4, 32], P('graph'), may hold values from 0 to 255
- send_count: int32 [8, 4], P('graph'), may hold values from 1 to 32, as said below
Outputs:
- input_grad: float32 [2048, 512], P('graph', 'batch')
- state_grad: float32 [2048, 512], P('graph', 'batch')
- gate_weight_grad: float32 [640, 128], replicated
- gate_bias_grad: float32 [128], replicated
- candidate_weight_grad: float32 [640, 64], replicated
- candidate_bias_grad: float32 [64], replicated
The draws below stay inside these ranges and needn't reach their ends.
Inputs may be any that keep to these rules, and one draw needn't show every extreme that they name: send_rows[p, j] lists rows of part p that part p + o_j reads; a row may stand in several lists or twice in one. The first send_count[p, j] entries of send_rows[p, j] are live; 32 is reached in every draw. `forward_tiles`: entries are zero or positive. `reverse_tiles`: entries are zero or positive. `forward_columns`: a value below 2 names a block of the part's own rows, a larger one a block of its rim. `reverse_columns`: as for forward_columns.
All inputs are finite; a program needn't handle non-finite values.
Results may differ from the reference program's by a relative error of at most 0.0055.
Values may be sent and summed in bfloat16 or wider, within the bound.
A program may use at most 64 MiB of HBM per device.

```python
import math
import jax
import jax.numpy as jnp
from jax import lax

HID = 64
INP = 64
KS = 5
TILE = 128
TPR = 3
REACH = 2
SLOT = 32
NODE_DEV = 256
NB = 2
HALO = 128
NCB = 3
PARTS_SIZE = 8
NODES = 2048
BATCH = 8
CH = 128


mean_degree = 8.0


def tile_values(key):
    mask_key, value_key = jax.random.split(key)
    shape = (NODES // TILE, TPR, TILE, TILE)
    chance = mean_degree / (TPR * TILE)
    present = jax.random.uniform(mask_key, shape, dtype=jnp.float32) < chance
    magnitude = jax.random.uniform(value_key, shape, dtype=jnp.float32, minval=0.05, maxval=0.2)
    return jnp.where(present, magnitude, 0.0).astype(jnp.bfloat16)


def draw_forward_tiles(key, part):
    return tile_values(jax.random.fold_in(key, 11))


def draw_reverse_tiles(key, part):
    return tile_values(jax.random.fold_in(key, 12))


def draw_send_count(key, part):
    count_key, spot_key = jax.random.split(jax.random.fold_in(key, 13))
    entries = PARTS_SIZE * 2 * REACH
    counts = jax.random.randint(count_key, (entries,), 1, SLOT + 1)
    spot = jax.random.randint(spot_key, (), 0, entries)
    filled = jnp.where(jnp.arange(entries) == spot, SLOT, counts)
    return filled.reshape(PARTS_SIZE, 2 * REACH).astype(jnp.int32)


def plant(values, rng, least, top_value):
    spot = [jax.random.randint(jax.random.fold_in(rng, axis), (), 0, length) for axis, length in enumerate(values.shape)]
    widest = values.shape.index(max(values.shape))
    beside = spot[:widest] + [(spot[widest] + 1) % values.shape[widest]] + spot[widest + 1:]
    return values.at[tuple(spot)].set(least).at[tuple(beside)].set(top_value)


def block_levels(rng, dims, cuts, least, largest):
    def one(dim, parts):
        draws = jax.random.uniform(jax.random.fold_in(jax.random.fold_in(rng, 6), dim), (parts,), jnp.float32, least / len(cuts), largest / len(cuts))
        return jnp.repeat(jnp.exp(draws), dims[dim] // parts).reshape((-1,) + (1,) * (len(dims) - dim - 1))

    loudness = one(*cuts[0])
    for cut in cuts[1:]:
        loudness = loudness * one(*cut)
    return loudness


def centred(key, shape, scale, bound, cuts=(), kind=jnp.bfloat16):
    values = scale * jax.random.normal(key, shape, jnp.float32)
    if cuts:
        values = values * block_levels(key, shape, cuts, -0.22, 0.18)
    return jnp.clip(values, -bound, bound).astype(kind)


def setup_inputs(seed: int = 0) -> dict:
    seeds = jax.random.split(jax.random.key(seed), 14)
    return {
        "layer_input": centred(seeds[0], (NODES, BATCH * INP), 1.0, 6.0, ((0, 8), (1, 4))),
        "hidden_state": centred(seeds[1], (NODES, BATCH * HID), 1.0, 6.0, ((0, 8), (1, 4))),
        "hidden_grad": centred(seeds[2], (NODES, BATCH * HID), 1.0, 6.0, ((0, 8), (1, 4))),
        "gate_weight": centred(seeds[3], (KS * CH, 2 * HID), (KS * CH) ** -0.5, 0.25),
        "gate_bias": centred(seeds[4], (2 * HID,), 0.5, 3.0, (), jnp.float32),
        "candidate_weight": centred(seeds[5], (KS * CH, HID), (KS * CH) ** -0.5, 0.25),
        "candidate_bias": centred(seeds[6], (HID,), 0.5, 3.0, (), jnp.float32),
        "forward_tiles": draw_forward_tiles(jax.random.fold_in(seeds[13], 71), 0),
        "forward_columns": plant(jax.random.randint(seeds[8], (NODES // TILE, TPR), 0, NCB), jax.random.fold_in(seeds[8], 1), 0, NCB - 1).astype(jnp.int32),
        "reverse_tiles": draw_reverse_tiles(jax.random.fold_in(seeds[13], 71), 0),
        "reverse_columns": plant(jax.random.randint(seeds[10], (NODES // TILE, TPR), 0, NCB), jax.random.fold_in(seeds[10], 1), 0, NCB - 1).astype(jnp.int32),
        "send_rows": plant(jax.random.randint(seeds[11], (PARTS_SIZE, 2 * REACH, SLOT), 0, NODE_DEV), jax.random.fold_in(seeds[11], 1), 0, NODE_DEV - 1).astype(jnp.int32),
        "send_count": draw_send_count(jax.random.fold_in(seeds[13], 71), 0),
    }


def rim_sources(send_rows, send_count):
    part_ids = jnp.arange(PARTS_SIZE, dtype=jnp.int32)
    offsets = jnp.array([(number // 2 + 1) * (1 - 2 * (number % 2)) for number in range(2 * REACH)], dtype=jnp.int32)
    source = part_ids[:, None] - offsets[None, :]
    inside = (source >= 0) & (source < PARTS_SIZE)
    clipped = jnp.clip(source, 0, PARTS_SIZE - 1).astype(jnp.int32)
    rim_sets = jnp.arange(2 * REACH, dtype=jnp.int32)
    listed = send_rows[clipped, rim_sets[None, :]]
    counts = send_count[clipped, rim_sets[None, :]]
    slot_ids = jnp.arange(SLOT, dtype=jnp.int32)
    valid_mask = inside[:, :, None] & (slot_ids[None, None, :] < counts[:, :, None])
    global_rows = (clipped[:, :, None] * NODE_DEV + listed).astype(jnp.int32)
    return (global_rows.reshape(PARTS_SIZE, HALO), valid_mask.reshape(PARTS_SIZE, HALO))

def spread(values, tiles, columns, sources):
    global_rows, valid_mask = sources
    feature_width = values.shape[1]

    def per_part(part_id):
        local_part = lax.dynamic_slice_in_dim(values, part_id * NODE_DEV, NODE_DEV, 0)
        rim_rows = jnp.where(valid_mask[part_id][:, None], values[global_rows[part_id]], jnp.zeros((), values.dtype))
        blocks = jnp.concatenate([local_part, rim_rows], 0).reshape(NCB, TILE, feature_width)
        own_tiles = lax.dynamic_slice_in_dim(tiles, part_id * NB, NB, 0)
        own_columns = lax.dynamic_slice_in_dim(columns, part_id * NB, NB, 0)
        picked = jnp.take(blocks, own_columns, axis=0)
        result = jnp.einsum('itac,itcm->iam', own_tiles.astype(jnp.float32), picked.astype(jnp.float32))
        return result.reshape(NODE_DEV, feature_width)
    return lax.map(per_part, jnp.arange(PARTS_SIZE, dtype=jnp.int32)).reshape(NODES, feature_width)

def gather_back(cotangents, tiles, columns, sources):
    global_rows, valid_mask = sources
    feature_width = cotangents.shape[1]

    def per_part(part_id):
        row_blocks = lax.dynamic_slice_in_dim(cotangents, part_id * NODE_DEV, NODE_DEV, 0).reshape(NB, TILE, feature_width)
        own_tiles = lax.dynamic_slice_in_dim(tiles, part_id * NB, NB, 0)
        own_columns = lax.dynamic_slice_in_dim(columns, part_id * NB, NB, 0)
        products = jnp.einsum('itac,iam->itcm', own_tiles.astype(jnp.float32), row_blocks.astype(jnp.float32))
        select = (own_columns[:, :, None] == jnp.arange(NCB, dtype=jnp.int32)[None, None, :]).astype(jnp.float32)
        blocks = jnp.einsum('itb,itcm->bcm', select, products, precision=lax.Precision.HIGHEST)
        blocks = blocks.reshape(NCB * TILE, feature_width)
        return (blocks[:NODE_DEV], blocks[NODE_DEV:])
    local_part, rim_rows = lax.map(per_part, jnp.arange(PARTS_SIZE, dtype=jnp.int32))
    rim_rows = rim_rows.reshape(PARTS_SIZE * HALO, feature_width)
    rim_rows = jnp.where(valid_mask.reshape(-1)[:, None], rim_rows, jnp.zeros((), rim_rows.dtype))
    return local_part.reshape(NODES, feature_width).at[global_rows.reshape(-1)].add(rim_rows)

def supports(values, graph_links, sources):
    forward_tiles, forward_columns, reverse_tiles, reverse_columns = graph_links
    base_field = values.astype(jnp.float32)
    first_forward = spread(values, forward_tiles, forward_columns, sources).astype(jnp.bfloat16)
    second_forward = (2.0 * spread(first_forward, forward_tiles, forward_columns, sources) - base_field).astype(jnp.bfloat16)
    first_reverse = spread(values, reverse_tiles, reverse_columns, sources).astype(jnp.bfloat16)
    second_reverse = (2.0 * spread(first_reverse, reverse_tiles, reverse_columns, sources) - base_field).astype(jnp.bfloat16)
    members = [values, first_forward, second_forward, first_reverse, second_reverse]
    return jnp.concatenate([member.reshape(-1, CH) for member in members], 1)

def back_supports(flat_grads, graph_links, sources):
    forward_tiles, forward_columns, reverse_tiles, reverse_columns = graph_links
    per_node = flat_grads.reshape(NODES, BATCH, KS, CH)
    members = [per_node[:, :, support].reshape(NODES, BATCH * CH) for support in range(KS)]
    first_forward = members[1] + 2.0 * gather_back(members[2].astype(jnp.bfloat16), forward_tiles, forward_columns, sources)
    first_reverse = members[3] + 2.0 * gather_back(members[4].astype(jnp.bfloat16), reverse_tiles, reverse_columns, sources)
    summed = members[0] - members[2] - members[4]
    summed = summed + gather_back(first_forward.astype(jnp.bfloat16), forward_tiles, forward_columns, sources)
    summed = summed + gather_back(first_reverse.astype(jnp.bfloat16), reverse_tiles, reverse_columns, sources)
    return summed.reshape(NODES * BATCH, CH)

def reference(layer_input, hidden_state, hidden_grad, gate_weight, gate_bias, candidate_weight, candidate_bias, forward_tiles, forward_columns, reverse_tiles, reverse_columns, send_rows, send_count):
    sources = rim_sources(send_rows, send_count)
    graph_links = (forward_tiles, forward_columns, reverse_tiles, reverse_columns)
    input_field = layer_input.reshape(NODES, BATCH, INP)
    hidden_field = hidden_state.reshape(NODES, BATCH, HID)
    stacked = jnp.concatenate([input_field, hidden_field], 2).reshape(NODES, BATCH * CH)
    gate_rows = supports(stacked, graph_links, sources)
    gate_values = jax.nn.sigmoid(jnp.dot(gate_rows, gate_weight, preferred_element_type=jnp.float32) + gate_bias)
    reset_gate = gate_values[:, :HID]
    update = gate_values[:, HID:]
    hidden_rows = hidden_state.reshape(-1, HID).astype(jnp.float32)
    gated = (reset_gate * hidden_rows).astype(jnp.bfloat16)
    candidate_input = jnp.concatenate([input_field, gated.reshape(NODES, BATCH, HID)], 2).reshape(NODES, BATCH * CH)
    candidate_rows = supports(candidate_input, graph_links, sources)
    candidate = jnp.tanh(jnp.dot(candidate_rows, candidate_weight, preferred_element_type=jnp.float32) + candidate_bias)
    cotangent = hidden_grad.reshape(-1, HID).astype(jnp.float32)
    update_grad = cotangent * (hidden_rows - candidate)
    candidate_grad = (cotangent * (1.0 - update) * (1.0 - candidate * candidate)).astype(jnp.bfloat16)
    norm_scale = 1.0 / math.sqrt(NODES * BATCH)
    candidate_sums = jnp.dot(candidate_rows.T, candidate_grad, preferred_element_type=jnp.float32) * norm_scale
    candidate_totals = lax.optimization_barrier(jnp.sum(candidate_grad.astype(jnp.float32), 0)) * norm_scale
    mixed_grad = back_supports(jnp.dot(candidate_grad, candidate_weight.T, preferred_element_type=jnp.float32), graph_links, sources)
    gated_grad = mixed_grad[:, INP:]
    reset_grad = gated_grad * hidden_rows
    gate_grad = jnp.concatenate([reset_grad * reset_gate * (1.0 - reset_gate), update_grad * update * (1.0 - update)], 1).astype(jnp.bfloat16)
    gate_sums = jnp.dot(gate_rows.T, gate_grad, preferred_element_type=jnp.float32) * norm_scale
    gate_totals = lax.optimization_barrier(jnp.sum(gate_grad.astype(jnp.float32), 0)) * norm_scale
    stacked_grad = back_supports(jnp.dot(gate_grad, gate_weight.T, preferred_element_type=jnp.float32), graph_links, sources)
    input_total = mixed_grad[:, :INP] + stacked_grad[:, :INP]
    hidden_total = cotangent * update + gated_grad * reset_gate + stacked_grad[:, INP:]
    return (input_total.reshape(NODES, BATCH * INP), hidden_total.reshape(NODES, BATCH * HID), gate_sums, gate_totals, candidate_sums, candidate_totals)
```

```python
import functools
import math

import jax
import jax.numpy as jnp
from jax import lax
from jax.experimental import pallas as pl
from jax.experimental.pallas import tpu as pltpu
from jax.sharding import PartitionSpec as P

HID = 64
KS = 5
CH = 128
MESH = pl.DeviceIdType.MESH
F32 = jnp.float32
BF16 = jnp.bfloat16


def rim_offsets(set_count):
    return [(number // 2 + 1) * (1 - 2 * (number % 2)) for number in range(set_count)]


def chunk_rows(rows, parts):
    return -(-(-(-rows // parts)) // 8) * 8


def nn(a, b):
    return lax.dot_general(a, b, (((1,), (0,)), ((), ())), preferred_element_type=F32)


def nt(a, b):
    return lax.dot_general(a, b, (((1,), (1,)), ((), ())), preferred_element_type=F32)


def tn(a, b):
    return lax.dot_general(a, b, (((0,), (0,)), ((), ())), preferred_element_type=F32)


class Rim:
    def __init__(self, n, me, offsets, sign, refs):
        self.n, self.me, self.sign = n, me, sign
        self.offsets = offsets
        self.out, self.into, self.send_sem, self.recv_sem = refs
        self.slot = self.out.shape[0] // len(offsets)

    def copy(self, j, device):
        rows = pl.ds(j * self.slot, self.slot)
        return pltpu.make_async_remote_copy(
            src_ref=self.out.at[rows],
            dst_ref=self.into.at[rows],
            send_sem=self.send_sem.at[j],
            recv_sem=self.recv_sem.at[j],
            device_id={"graph": device},
            device_id_type=MESH,
        )

    def each(self, sign, act):
        for j, offset in enumerate(self.offsets):
            other = self.me + sign * offset
            pl.when((other >= 0) & (other < self.n))(functools.partial(act, j, other))

    def start(self, value):
        self.out[...] = value.astype(BF16)
        self.each(self.sign, lambda j, other: self.copy(j, other).start())

    def arrived(self):
        self.each(-self.sign, lambda j, other: self.copy(j, other).wait_recv())
        return self.into[...]

    def finish(self):
        self.each(self.sign, lambda j, other: self.copy(j, other).wait_send())


class Total:
    def __init__(self, nb, ng, mb, mg, refs):
        self.nb, self.ng, self.mb, self.mg = nb, ng, mb, mg
        self.stage, self.mine, self.got, self.part, self.heard, self.slab, self.out = refs[:7]
        self.sems = refs[7:]
        self.started = []

    def copy(self, phase, axis, count, me, src, dst):
        send_sem, recv_sem = self.sems[2 * phase], self.sems[2 * phase + 1]
        for d in range(1, count):
            other = lax.rem(me + d, count)
            c = pltpu.make_async_remote_copy(
                src_ref=src(other),
                dst_ref=dst(d),
                send_sem=send_sem.at[d],
                recv_sem=recv_sem.at[d],
                device_id={axis: other},
                device_id_type=MESH,
            )
            c.start()
            self.started.append(c)
        return self.started[len(self.started) - (count - 1) :] if count > 1 else []

    def phase1(self):
        self.mine[...] = self.stage[...].reshape(self.mine.shape).astype(BF16)
        self.wait = self.copy(
            0, "batch", self.nb, self.mb, lambda o: self.mine.at[o], lambda d: self.got.at[d]
        )

    def phase2(self):
        for c in self.wait:
            c.wait_recv()
        total = self.mine[self.mb].astype(F32)
        for d in range(1, self.nb):
            total += self.got[d].astype(F32)
        self.part[...] = total.reshape(self.part.shape).astype(BF16)
        self.wait = self.copy(
            1, "graph", self.ng, self.mg, lambda o: self.part.at[o], lambda d: self.heard.at[d]
        )

    def phase3(self):
        for c in self.wait:
            c.wait_recv()
        total = self.part[self.mg].astype(F32)
        for d in range(1, self.ng):
            total += self.heard[d].astype(F32)
        self.slab[self.mg] = total.astype(BF16)
        self.wait = self.copy(
            2,
            "graph",
            self.ng,
            self.mg,
            lambda o: self.slab.at[self.mg],
            lambda d: self.slab.at[self.mg],
        )

    def phase4(self):
        for c in self.wait:
            c.wait_recv()
        self.wait = self.copy(
            3, "batch", self.nb, self.mb, lambda o: self.slab, lambda d: self.out.at[self.mb]
        )
        self.out[self.mb] = self.slab[...]

    def phase5(self):
        for c in self.wait:
            c.wait_recv()

    def finish(self):
        for c in self.started:
            c.wait_send()


def step_kernel(
    ng,
    nb,
    counts,
    x_ref,
    h_ref,
    cot_ref,
    wg_ref,
    bias_ref,
    wc_ref,
    ft_ref,
    fc_ref,
    rt_ref,
    rc_ref,
    list_ref,
    list_row_ref,
    in_grad_ref,
    state_grad_ref,
    total1_ref,
    total2_ref,
    *scratch,
):
    set_count, slot = counts
    mg, mb = lax.axis_index("graph"), lax.axis_index("batch")
    nodes = x_ref.shape[0]
    w = x_ref.shape[1]
    half = w // 2
    tile = ft_ref.shape[2]
    rows_i, tpr = ft_ref.shape[:2]
    halo = set_count * slot
    blocks = (nodes + halo) // tile
    offsets = rim_offsets(set_count)
    wgx, wcx, a_ref, at_ref, sup_ref, cand_ref, g_ref = scratch[:7]
    rest = list(scratch[7:])
    signs = (1, 1, 1, 1, -1, -1, -1, -1)
    rims = [Rim(ng, mg, offsets, signs[e], rest[4 * e : 4 * e + 4]) for e in range(8)]
    rest = rest[32:]
    sum1 = Total(nb, ng, mb, mg, rest[:6] + [total1_ref] + rest[6:14])
    rest = rest[14:]
    sum2 = Total(nb, ng, mb, mg, rest[:6] + [total2_ref] + rest[6:14])

    for rim in rims:
        rim.into[...] = jnp.zeros(rim.into.shape, BF16)
    barrier = pltpu.get_barrier_semaphore()
    for d in range(1, ng):
        pl.semaphore_signal(
            barrier, inc=1, device_id={"graph": lax.rem(mg + d, ng)}, device_id_type=MESH
        )
    for d in range(1, nb):
        pl.semaphore_signal(
            barrier, inc=1, device_id={"batch": lax.rem(mb + d, nb)}, device_id_type=MESH
        )

    listed = list_ref[...]
    sel = jnp.where(
        lax.broadcasted_iota(jnp.int32, (halo, nodes), 1) == listed, 1.0, 0.0
    ).astype(BF16)
    sel_t = jnp.where(
        lax.broadcasted_iota(jnp.int32, (nodes, halo), 0) == list_row_ref[...], 1.0, 0.0
    ).astype(BF16)

    x = x_ref[...]
    h = h_ref[...]
    sup_ref[:, :w] = x
    sup_ref[:, w : 2 * w] = h
    values = sup_ref[:, : 2 * w]
    first = nn(sel, values)
    pl.semaphore_wait(barrier, ng + nb - 2)
    rims[0].start(first)

    for side, (tiles, cols) in enumerate(((ft_ref, fc_ref), (rt_ref, rc_ref))):
        for i in range(rows_i):
            for b in range(blocks):
                acc = None
                for t in range(tpr):
                    keep = (cols[i, t] == b).astype(F32)
                    term = tiles[i, t].astype(F32) * keep
                    acc = term if acc is None else acc + term
                r0 = side * nodes + i * tile
                a_ref[r0 : r0 + tile, b * tile : (b + 1) * tile] = acc.astype(BF16)
                at_ref[b * tile : (b + 1) * tile, r0 : r0 + tile] = acc.T.astype(BF16)

    own = a_ref[:, :nodes]
    local13 = nn(own, values)

    def widen(weight, columns, outs):
        pieces = []
        for k in range(KS):
            low = weight[k * CH : k * CH + half]
            high = weight[k * CH + half : (k + 1) * CH]
            pieces += [low, low, high, high]
        tall = jnp.concatenate(pieces, 0)
        i = lax.broadcasted_iota(jnp.int32, (columns, outs), 0)
        j = lax.broadcasted_iota(jnp.int32, (columns, outs), 1)
        pick = jnp.where(i == (j // w) * half + j % half, 1.0, 0.0).astype(BF16)
        wide = nn(tall, pick)
        i = lax.broadcasted_iota(jnp.int32, wide.shape, 0)
        j = lax.broadcasted_iota(jnp.int32, wide.shape, 1)
        return jnp.where((i // half) % 2 == (j // half) % 2, wide, 0.0).astype(BF16)

    wgx[...] = widen(wg_ref[...], 2 * HID, 2 * w)
    wcx[...] = widen(wc_ref[...], HID, w)

    s13 = local13 + nn(a_ref[:, nodes:], rims[0].arrived())
    s1 = s13[:nodes].astype(BF16)
    s3 = s13[nodes:].astype(BF16)
    sup_ref[:, 2 * w : 4 * w] = s1
    sup_ref[:, 6 * w : 8 * w] = s3
    rims[1].start(jnp.concatenate([nn(sel, s1), nn(sel, s3)], 1))
    base = values.astype(F32)
    l2 = nn(a_ref[:nodes, :nodes], s1)
    l4 = nn(a_ref[nodes:, :nodes], s3)
    pre = nn(values, wgx[: 2 * w]) + nn(s1, wgx[2 * w : 4 * w]) + nn(s3, wgx[6 * w : 8 * w])
    rim = rims[1].arrived()
    l2 += nn(a_ref[:nodes, nodes:], rim[:, : 2 * w])
    l4 += nn(a_ref[nodes:, nodes:], rim[:, 2 * w :])
    s2 = (2.0 * l2 - base).astype(BF16)
    s4 = (2.0 * l4 - base).astype(BF16)
    sup_ref[:, 4 * w : 6 * w] = s2
    sup_ref[:, 8 * w :] = s4
    pre += nn(s2, wgx[4 * w : 6 * w]) + nn(s4, wgx[8 * w :])
    hf = h.astype(F32)
    reset = jax.nn.sigmoid(pre[:, :w] + bias_ref[0:1, :])
    update = jax.nn.sigmoid(pre[:, w:] + bias_ref[1:2, :])

    gated = (reset * hf).astype(BF16)
    rims[2].start(nn(sel, gated))
    cand_ref[:, :w] = gated
    l13 = nn(own, gated)
    cpre = nn(gated, wcx[w : 2 * w])
    for k in range(KS):
        cpre += nn(sup_ref[:, 2 * k * w : (2 * k + 1) * w], wcx[2 * k * w : (2 * k + 1) * w])
    l13 += nn(a_ref[:, nodes:], rims[2].arrived())
    t1 = l13[:nodes].astype(BF16)
    t3 = l13[nodes:].astype(BF16)
    rims[3].start(jnp.concatenate([nn(sel, t1), nn(sel, t3)], 1))
    cand_ref[:, w : 2 * w] = t1
    cand_ref[:, 3 * w : 4 * w] = t3
    l2 = nn(a_ref[:nodes, :nodes], t1)
    l4 = nn(a_ref[nodes:, :nodes], t3)
    cpre += nn(t1, wcx[3 * w : 4 * w]) + nn(t3, wcx[7 * w : 8 * w])
    rim = rims[3].arrived()
    l2 += nn(a_ref[:nodes, nodes:], rim[:, :w])
    l4 += nn(a_ref[nodes:, nodes:], rim[:, w:])
    gatedf = gated.astype(F32)
    t2 = (2.0 * l2 - gatedf).astype(BF16)
    t4 = (2.0 * l4 - gatedf).astype(BF16)
    cand_ref[:, 2 * w : 3 * w] = t2
    cand_ref[:, 4 * w :] = t4
    cpre += nn(t2, wcx[5 * w : 6 * w]) + nn(t4, wcx[9 * w :])
    cand = jnp.tanh(cpre + bias_ref[2:3, :])

    cot = cot_ref[...].astype(F32)
    update_grad = cot * (hf - cand)
    cg = (cot * (1.0 - update) * (1.0 - cand * cand)).astype(BF16)
    gu = (update_grad * update * (1.0 - update)).astype(BF16)

    def cand_cot(k, part):
        r0 = (2 * k + part) * w
        return nt(cg, wcx[r0 : r0 + w])

    c2, c4 = cand_cot(2, 1), cand_cot(4, 1)
    c2b, c4b = c2.astype(BF16), c4.astype(BF16)
    atf, atr = at_ref[:, :nodes], at_ref[:, nodes:]
    rims[4].start(jnp.concatenate([nn(atf[nodes:], c2b), nn(atr[nodes:], c4b)], 1))
    f1 = cand_cot(1, 1) + 2.0 * nn(atf[:nodes], c2b)
    f3 = cand_cot(3, 1) + 2.0 * nn(atr[:nodes], c4b)
    rest_h = cand_cot(0, 1) - c2 - c4

    low = lax.broadcasted_iota(jnp.int32, (half, w), 1) < half

    def fold(m):
        t = jnp.where(low[:1] if m[0].shape[0] == 1 else low, m[0], m[1])
        return t + pltpu.roll(t, half, 1)

    def colsum(v):
        s = jnp.sum(v.astype(F32), 0, keepdims=True)
        s = jnp.broadcast_to(s, (8, w))
        return s + pltpu.roll(s, half, 1)

    def both(mx, mh):
        return [fold((mx[:half], mx[half:])), fold((mh[:half], mh[half:]))]

    low8 = low[:8]
    for k in range(KS):
        sx = sup_ref[:, 2 * k * w : (2 * k + 1) * w]
        sh = sup_ref[:, (2 * k + 1) * w : (2 * k + 2) * w]
        th = cand_ref[:, k * w : (k + 1) * w]
        yc = both(tn(sx, cg), tn(th, cg))
        yu = both(tn(sx, gu), tn(sh, gu))
        for part in range(2):
            r0 = k * CH + part * half
            sum1.stage[r0 : r0 + half] = jnp.where(low, yc[part], yu[part])
    used = KS * CH
    sum1.stage[used : used + 8] = jnp.where(low8, colsum(cg), colsum(gu))
    if sum1.stage.shape[0] > used + 8:
        sum1.stage[used + 8 :] = jnp.zeros((sum1.stage.shape[0] - used - 8, w), F32)
    sum1.phase1()

    back = nn(sel_t, rims[4].arrived())
    f1b = (f1 + 2.0 * back[:, :w]).astype(BF16)
    f3b = (f3 + 2.0 * back[:, w:]).astype(BF16)
    rims[5].start(nn(atf[nodes:], f1b) + nn(atr[nodes:], f3b))
    rest_h += nn(atf[:nodes], f1b) + nn(atr[:nodes], f3b)
    for k in range(KS):
        rows = slice(2 * k * w, 2 * (k + 1) * w)
        part = nt(gu, wgx[rows, w:])
        g_ref[:, 2 * k * w : (2 * k + 1) * w] = part[:, :w] + cand_cot(k, 0)
        g_ref[:, (2 * k + 1) * w : 2 * (k + 1) * w] = part[:, w:]
    sum1.phase2()
    gated_grad = rest_h + nn(sel_t, rims[5].arrived())

    gr = (gated_grad * hf * reset * (1.0 - reset)).astype(BF16)

    def gate_cot(k):
        cols = slice(2 * k * w, 2 * (k + 1) * w)
        return g_ref[:, cols] + nt(gr, wgx[cols, :w])

    g2, g4 = gate_cot(2), gate_cot(4)
    g2b, g4b = g2.astype(BF16), g4.astype(BF16)
    rims[6].start(jnp.concatenate([nn(atf[nodes:], g2b), nn(atr[nodes:], g4b)], 1))
    f1 = gate_cot(1) + 2.0 * nn(atf[:nodes], g2b)
    f3 = gate_cot(3) + 2.0 * nn(atr[:nodes], g4b)
    rest_all = gate_cot(0) - g2 - g4
    folded = []
    for k in range(KS):
        sx = sup_ref[:, 2 * k * w : (2 * k + 1) * w]
        sh = sup_ref[:, (2 * k + 1) * w : (2 * k + 2) * w]
        folded += both(tn(sx, gr), tn(sh, gr))
    for m in range(KS):
        sum2.stage[m * half : (m + 1) * half] = jnp.where(low, folded[m], folded[m + KS])
    used = KS * half
    sum2.stage[used : used + 8] = colsum(gr)
    if sum2.stage.shape[0] > used + 8:
        sum2.stage[used + 8 :] = jnp.zeros((sum2.stage.shape[0] - used - 8, w), F32)
    sum2.phase1()
    sum1.phase3()

    back = nn(sel_t, rims[6].arrived())
    f1b = (f1 + 2.0 * back[:, : 2 * w]).astype(BF16)
    f3b = (f3 + 2.0 * back[:, 2 * w :]).astype(BF16)
    rims[7].start(nn(atf[nodes:], f1b) + nn(atr[nodes:], f3b))
    rest_all += nn(atf[:nodes], f1b) + nn(atr[:nodes], f3b)
    sum2.phase2()
    sum1.phase4()
    rest_all += nn(sel_t, rims[7].arrived())
    sum2.phase3()
    in_grad_ref[...] = rest_all[:, :w]
    state_grad_ref[...] = cot * update + gated_grad * reset + rest_all[:, w:]
    sum2.phase4()
    sum1.phase5()
    sum2.phase5()
    for rim in rims:
        rim.finish()
    sum1.finish()
    sum2.finish()


def on_device(
    layer_input,
    hidden_state,
    hidden_grad,
    gate_weight,
    gate_bias,
    candidate_weight,
    candidate_bias,
    forward_tiles,
    forward_columns,
    reverse_tiles,
    reverse_columns,
    send_rows,
    send_count,
):
    ng, nb = lax.axis_size("graph"), lax.axis_size("batch")
    nodes, w = layer_input.shape
    set_count, slot = send_rows.shape[1:]
    halo = set_count * slot
    ids = jnp.arange(slot, dtype=jnp.int32)
    listed = jnp.where(ids[None, :] < send_count[0][:, None], send_rows[0], -1).reshape(halo, 1)
    reset_bias, update_bias = gate_bias[:HID], gate_bias[HID:]
    bias = jnp.stack(
        [jnp.concatenate([b, b]) for b in (reset_bias, update_bias, candidate_bias)]
    )
    r1 = chunk_rows(KS * CH + 8, ng * nb)
    r2 = chunk_rows(KS * CH // 2 + 8, ng * nb)
    widths = (2 * w, 4 * w, w, 2 * w, 2 * w, w, 4 * w, 2 * w)
    scratch = [
        pltpu.VMEM((KS * 2 * w, 2 * w), BF16),
        pltpu.VMEM((KS * 2 * w, w), BF16),
        pltpu.VMEM((2 * nodes, nodes + halo), BF16),
        pltpu.VMEM((nodes + halo, 2 * nodes), BF16),
        pltpu.VMEM((nodes, KS * 2 * w), BF16),
        pltpu.VMEM((nodes, KS * w), BF16),
        pltpu.VMEM((nodes, KS * 2 * w), F32),
    ]
    dma = lambda count: pltpu.SemaphoreType.DMA((count,))
    for width in widths:
        scratch += [
            pltpu.VMEM((halo, width), BF16),
            pltpu.VMEM((halo, width), BF16),
            dma(set_count),
            dma(set_count),
        ]
    for r in (r1, r2):
        scratch += [
            pltpu.VMEM((nb * ng * r, w), F32),
            pltpu.VMEM((nb, ng * r, w), BF16),
            pltpu.VMEM((nb, ng * r, w), BF16),
            pltpu.VMEM((ng, r, w), BF16),
            pltpu.VMEM((ng, r, w), BF16),
            pltpu.VMEM((ng, r, w), BF16),
            dma(nb),
            dma(nb),
            dma(ng),
            dma(ng),
            dma(ng),
            dma(ng),
            dma(nb),
            dma(nb),
        ]
    vmem = pl.BlockSpec(memory_space=pltpu.VMEM)
    smem = pl.BlockSpec(memory_space=pltpu.SMEM)
    input_grad, state_grad, total1, total2 = pl.pallas_call(
        functools.partial(step_kernel, ng, nb, (set_count, slot)),
        name="gru_backward",
        out_shape=(
            jax.ShapeDtypeStruct((nodes, w), F32),
            jax.ShapeDtypeStruct((nodes, w), F32),
            jax.ShapeDtypeStruct((nb, ng, r1, w), BF16),
            jax.ShapeDtypeStruct((nb, ng, r2, w), BF16),
        ),
        in_specs=[vmem] * 7 + [smem, vmem, smem, vmem, vmem],
        out_specs=(vmem,) * 4,
        scratch_shapes=scratch,
        compiler_params=pltpu.CompilerParams(
            collective_id=0, has_side_effects=True, vmem_limit_bytes=56 * 1024 * 1024
        ),
    )(
        layer_input,
        hidden_state,
        hidden_grad,
        gate_weight,
        bias,
        candidate_weight,
        forward_tiles,
        forward_columns,
        reverse_tiles,
        reverse_columns,
        listed,
        listed.reshape(1, halo),
    )
    samples = w // HID
    scale = 1.0 / math.sqrt(nodes * ng * samples * nb)
    total1 = total1.reshape(-1, w).astype(F32) * scale
    total2 = total2.reshape(-1, w).astype(F32) * scale
    used, used2 = KS * CH, KS * CH // 2
    reset_grads = jnp.concatenate([total2[:used2, :HID], total2[:used2, HID:]], 0)
    return (
        input_grad,
        state_grad,
        jnp.concatenate([reset_grads, total1[:used, HID:]], 1),
        jnp.concatenate([total2[used2, :HID], total1[used, HID:]]),
        total1[:used, :HID],
        total1[used, :HID],
    )


def solution(mesh):
    placed = (
        P("graph", "batch"),
        P("graph", "batch"),
        P("graph", "batch"),
        P(),
        P(),
        P(),
        P(),
        P("graph", None, None, None),
        P("graph", None),
        P("graph", None, None, None),
        P("graph", None),
        P("graph", None, None),
        P("graph", None),
    )
    return jax.shard_map(
        on_device,
        mesh=mesh,
        in_specs=placed,
        out_specs=(P("graph", "batch"), P("graph", "batch"), P(), P(), P(), P()),
        check_vma=False,
    )
```

```python
import functools
import math

import jax
import jax.numpy as jnp
from jax import lax
from jax.experimental import pallas as pl
from jax.experimental.pallas import tpu as pltpu
from jax.sharding import PartitionSpec as P

HID = 64
KS = 5
CH = 128
MESH = pl.DeviceIdType.MESH
F32 = jnp.float32
BF16 = jnp.bfloat16


def rim_offsets(set_count):
    return [(number // 2 + 1) * (1 - 2 * (number % 2)) for number in range(set_count)]


def chunk_rows(rows, parts):
    return -(-(-(-rows // parts)) // 8) * 8


def nn(a, b):
    return lax.dot_general(a, b, (((1,), (0,)), ((), ())), preferred_element_type=F32)


def nt(a, b):
    return lax.dot_general(a, b, (((1,), (1,)), ((), ())), preferred_element_type=F32)


def tn(a, b):
    return lax.dot_general(a, b, (((0,), (0,)), ((), ())), preferred_element_type=F32)


class Rim:
    def __init__(self, n, me, offsets, sign, refs):
        self.n, self.me, self.sign = n, me, sign
        self.offsets = offsets
        self.out, self.into, self.send_sem, self.recv_sem = refs
        self.slot = self.out.shape[0] // len(offsets)

    def copy(self, j, device):
        rows = pl.ds(j * self.slot, self.slot)
        return pltpu.make_async_remote_copy(
            src_ref=self.out.at[rows],
            dst_ref=self.into.at[rows],
            send_sem=self.send_sem.at[j],
            recv_sem=self.recv_sem.at[j],
            device_id={"graph": device},
            device_id_type=MESH,
        )

    def each(self, sign, act):
        for j, offset in enumerate(self.offsets):
            other = self.me + sign * offset
            pl.when((other >= 0) & (other < self.n))(functools.partial(act, j, other))

    def start(self, value):
        self.out[...] = value.astype(BF16)
        self.each(self.sign, lambda j, other: self.copy(j, other).start())

    def arrived(self):
        self.each(-self.sign, lambda j, other: self.copy(j, other).wait_recv())
        return self.into[...]

    def finish(self):
        self.each(self.sign, lambda j, other: self.copy(j, other).wait_send())


class Total:
    def __init__(self, nb, ng, mb, mg, refs):
        self.nb, self.ng, self.mb, self.mg = nb, ng, mb, mg
        self.stage, self.mine, self.got, self.part, self.heard, self.slab, self.out = refs[:7]
        self.sems = refs[7:]
        self.started = []

    def copy(self, phase, axis, count, me, src, dst):
        send_sem, recv_sem = self.sems[2 * phase], self.sems[2 * phase + 1]
        for d in range(1, count):
            other = lax.rem(me + d, count)
            c = pltpu.make_async_remote_copy(
                src_ref=src(other),
                dst_ref=dst(d),
                send_sem=send_sem.at[d],
                recv_sem=recv_sem.at[d],
                device_id={axis: other},
                device_id_type=MESH,
            )
            c.start()
            self.started.append(c)
        return self.started[len(self.started) - (count - 1) :] if count > 1 else []

    def phase1(self):
        self.mine[...] = self.stage[...].reshape(self.mine.shape).astype(BF16)
        self.wait = self.copy(
            0, "batch", self.nb, self.mb, lambda o: self.mine.at[o], lambda d: self.got.at[d]
        )

    def phase2(self):
        for c in self.wait:
            c.wait_recv()
        total = self.mine[self.mb].astype(F32)
        for d in range(1, self.nb):
            total += self.got[d].astype(F32)
        self.part[...] = total.reshape(self.part.shape).astype(BF16)
        self.wait = self.copy(
            1, "graph", self.ng, self.mg, lambda o: self.part.at[o], lambda d: self.heard.at[d]
        )

    def phase3(self):
        for c in self.wait:
            c.wait_recv()
        total = self.part[self.mg].astype(F32)
        for d in range(1, self.ng):
            total += self.heard[d].astype(F32)
        self.slab[self.mg] = total.astype(BF16)
        self.wait = self.copy(
            2,
            "graph",
            self.ng,
            self.mg,
            lambda o: self.slab.at[self.mg],
            lambda d: self.slab.at[self.mg],
        )

    def phase4(self):
        for c in self.wait:
            c.wait_recv()
        self.wait = self.copy(
            3, "batch", self.nb, self.mb, lambda o: self.slab, lambda d: self.out.at[self.mb]
        )
        self.out[self.mb] = self.slab[...]

    def phase5(self):
        for c in self.wait:
            c.wait_recv()

    def finish(self):
        for c in self.started:
            c.wait_send()


class Direct:
    def __init__(self, nb, ng, mb, mg, refs):
        self.n, self.ng = nb * ng, ng
        self.me = mb * ng + mg
        self.stage, self.mine, self.got, self.out = refs[:4]
        self.sems = refs[4:]
        self.started = []

    def copy(self, phase, src, dst):
        send_sem, recv_sem = self.sems[2 * phase], self.sems[2 * phase + 1]
        self.wait = []
        for d in range(1, self.n):
            other = lax.rem(self.me + d, self.n)
            c = pltpu.make_async_remote_copy(
                src_ref=src(other),
                dst_ref=dst(d),
                send_sem=send_sem.at[d],
                recv_sem=recv_sem.at[d],
                device_id={"graph": lax.rem(other, self.ng), "batch": lax.div(other, self.ng)},
                device_id_type=MESH,
            )
            c.start()
            self.wait.append(c)
        self.started += self.wait

    def phase1(self):
        self.mine[...] = self.stage[...].reshape(self.mine.shape).astype(BF16)
        self.copy(0, lambda o: self.mine.at[o], lambda d: self.got.at[d])

    def phase2(self):
        for c in self.wait:
            c.wait_recv()
        total = self.mine[self.me].astype(F32)
        for d in range(1, self.n):
            total += self.got[d].astype(F32)
        self.out[self.me] = total.astype(BF16)
        self.copy(1, lambda o: self.out.at[self.me], lambda d: self.out.at[self.me])

    def phase3(self):
        for c in self.wait:
            c.wait_recv()

    def finish(self):
        for c in self.started:
            c.wait_send()


def step_kernel(
    ng,
    nb,
    scale,
    x_ref,
    h_ref,
    cot_ref,
    wg_ref,
    gate_bias_ref,
    wc_ref,
    cand_bias_ref,
    ft_ref,
    fc_ref,
    rt_ref,
    rc_ref,
    list_ref,
    count_ref,
    in_grad_ref,
    state_grad_ref,
    gate_grad_ref,
    gate_bias_grad_ref,
    cand_grad_ref,
    cand_bias_grad_ref,
    *scratch,
):
    set_count, slot = list_ref.shape[1:]
    mg, mb = lax.axis_index("graph"), lax.axis_index("batch")
    nodes = x_ref.shape[0]
    w = x_ref.shape[1]
    half = w // 2
    tile = ft_ref.shape[2]
    rows_i, tpr = ft_ref.shape[:2]
    halo = set_count * slot
    blocks = (nodes + halo) // tile
    offsets = rim_offsets(set_count)
    wgx, wcx, a_ref, at_ref, sup_ref, cand_ref, g_ref = scratch[:7]
    rest = list(scratch[7:])
    signs = (1, 1, 1, 1, -1, -1, -1, -1)
    rims = [Rim(ng, mg, offsets, signs[e], rest[4 * e : 4 * e + 4]) for e in range(8)]
    rest = rest[32:]
    sum1 = Total(nb, ng, mb, mg, rest[:15])
    sum2 = Direct(nb, ng, mb, mg, rest[15:])

    for rim in rims:
        rim.into[...] = jnp.zeros(rim.into.shape, BF16)
    barrier = pltpu.get_barrier_semaphore()
    n, me = nb * ng, mb * ng + mg
    for d in range(1, n):
        other = lax.rem(me + d, n)
        pl.semaphore_signal(
            barrier,
            inc=1,
            device_id={"graph": lax.rem(other, ng), "batch": lax.div(other, ng)},
            device_id_type=MESH,
        )

    ids = lax.broadcasted_iota(jnp.int32, (1, slot), 1)
    listed = jnp.concatenate(
        [jnp.where(ids < count_ref[0, j], list_ref[0, j : j + 1, :], -1) for j in range(set_count)],
        1,
    )
    sel_f = jnp.where(
        lax.broadcasted_iota(jnp.int32, (nodes, halo), 0)
        == jnp.broadcast_to(listed, (nodes, halo)),
        1.0,
        0.0,
    )
    sel_t = sel_f.astype(BF16)
    sel = sel_f.T.astype(BF16)

    x = x_ref[...]
    h = h_ref[...]
    sup_ref[:, :w] = x
    sup_ref[:, w : 2 * w] = h
    values = sup_ref[:, : 2 * w]
    first = nn(sel, values)

    for side, (tiles, cols) in enumerate(((ft_ref, fc_ref), (rt_ref, rc_ref))):
        for i in range(rows_i):
            for b in range(blocks):
                acc = None
                for t in range(tpr):
                    keep = (cols[i, t] == b).astype(F32)
                    term = tiles[i, t].astype(F32) * keep
                    acc = term if acc is None else acc + term
                r0 = side * nodes + i * tile
                a_ref[r0 : r0 + tile, b * tile : (b + 1) * tile] = acc.astype(BF16)
                at_ref[b * tile : (b + 1) * tile, r0 : r0 + tile] = acc.T.astype(BF16)

    pl.semaphore_wait(barrier, n - 1)
    rims[0].start(first)

    own = a_ref[:, :nodes]
    af_sent = nn(sel, a_ref[:nodes, :]).astype(BF16)
    ar_sent = nn(sel, a_ref[nodes:, :]).astype(BF16)
    sent13 = [nn(m[:, :nodes], values) for m in (af_sent, ar_sent)]
    local13 = nn(own, values)

    def widen(weight, columns, outs):
        pieces = []
        for k in range(KS):
            low = weight[k * CH : k * CH + half]
            high = weight[k * CH + half : (k + 1) * CH]
            pieces += [low, low, high, high]
        tall = jnp.concatenate(pieces, 0)
        i = lax.broadcasted_iota(jnp.int32, (columns, outs), 0)
        j = lax.broadcasted_iota(jnp.int32, (columns, outs), 1)
        pick = jnp.where(i == (j // w) * half + j % half, 1.0, 0.0).astype(BF16)
        wide = nn(tall, pick)
        i = lax.broadcasted_iota(jnp.int32, wide.shape, 0)
        j = lax.broadcasted_iota(jnp.int32, wide.shape, 1)
        return jnp.where((i // half) % 2 == (j // half) % 2, wide, 0.0).astype(BF16)

    wgx[...] = widen(wg_ref[...], 2 * HID, 2 * w)
    wcx[...] = widen(wc_ref[...].astype(F32).T.astype(BF16), HID, w)
    atf, atr = at_ref[:, :nodes], at_ref[:, nodes:]
    af_back = nn(atf[nodes:], sel_t).astype(BF16)
    ar_back = nn(atr[nodes:], sel_t).astype(BF16)

    gate_bias = jnp.broadcast_to(gate_bias_ref[...], (8, w))
    turned = pltpu.roll(gate_bias, half, 1)
    low8 = lax.broadcasted_iota(jnp.int32, (8, w), 1) < half
    reset_bias = jnp.where(low8, gate_bias, turned)[:1]
    update_bias = jnp.where(low8, turned, gate_bias)[:1]
    cand_bias = jnp.concatenate([cand_bias_ref[...]] * 2, 1)

    rim = rims[0].arrived()
    sent = [m + nn(a[:, nodes:], rim) for m, a in zip(sent13, (af_sent, ar_sent))]
    rims[1].start(jnp.concatenate(sent, 1))
    s13 = local13 + nn(a_ref[:, nodes:], rim)
    s1 = s13[:nodes].astype(BF16)
    s3 = s13[nodes:].astype(BF16)
    sup_ref[:, 2 * w : 4 * w] = s1
    sup_ref[:, 6 * w : 8 * w] = s3
    base = values.astype(F32)
    l2 = nn(a_ref[:nodes, :nodes], s1)
    l4 = nn(a_ref[nodes:, :nodes], s3)
    pre = nn(values, wgx[: 2 * w]) + nn(s1, wgx[2 * w : 4 * w]) + nn(s3, wgx[6 * w : 8 * w])
    rim = rims[1].arrived()
    l2 += nn(a_ref[:nodes, nodes:], rim[:, : 2 * w])
    l4 += nn(a_ref[nodes:, nodes:], rim[:, 2 * w :])
    s2 = (2.0 * l2 - base).astype(BF16)
    s4 = (2.0 * l4 - base).astype(BF16)
    sup_ref[:, 4 * w : 6 * w] = s2
    sup_ref[:, 8 * w :] = s4
    pre += nn(s2, wgx[4 * w : 6 * w]) + nn(s4, wgx[8 * w :])
    hf = h.astype(F32)
    reset = jax.nn.sigmoid(pre[:, :w] + reset_bias)
    update = jax.nn.sigmoid(pre[:, w:] + update_bias)

    gated = (reset * hf).astype(BF16)
    rims[2].start(nn(sel, gated))
    cand_ref[:, :w] = gated
    sent13 = [nn(m[:, :nodes], gated) for m in (af_sent, ar_sent)]
    l13 = nn(own, gated)
    cpre = nn(gated, wcx[w : 2 * w])
    for k in range(KS):
        cpre += nn(sup_ref[:, 2 * k * w : (2 * k + 1) * w], wcx[2 * k * w : (2 * k + 1) * w])
    rim = rims[2].arrived()
    sent = [m + nn(a[:, nodes:], rim) for m, a in zip(sent13, (af_sent, ar_sent))]
    rims[3].start(jnp.concatenate(sent, 1))
    l13 += nn(a_ref[:, nodes:], rim)
    t1 = l13[:nodes].astype(BF16)
    t3 = l13[nodes:].astype(BF16)
    cand_ref[:, w : 2 * w] = t1
    cand_ref[:, 3 * w : 4 * w] = t3
    l2 = nn(a_ref[:nodes, :nodes], t1)
    l4 = nn(a_ref[nodes:, :nodes], t3)
    cpre += nn(t1, wcx[3 * w : 4 * w]) + nn(t3, wcx[7 * w : 8 * w])
    rim = rims[3].arrived()
    l2 += nn(a_ref[:nodes, nodes:], rim[:, :w])
    l4 += nn(a_ref[nodes:, nodes:], rim[:, w:])
    gatedf = gated.astype(F32)
    t2 = (2.0 * l2 - gatedf).astype(BF16)
    t4 = (2.0 * l4 - gatedf).astype(BF16)
    cand_ref[:, 2 * w : 3 * w] = t2
    cand_ref[:, 4 * w :] = t4
    cpre += nn(t2, wcx[5 * w : 6 * w]) + nn(t4, wcx[9 * w :])
    cand = jnp.tanh(cpre + cand_bias)

    cot = cot_ref[...].astype(F32)
    update_grad = cot * (hf - cand)
    cg = (cot * (1.0 - update) * (1.0 - cand * cand)).astype(BF16)
    gu = (update_grad * update * (1.0 - update)).astype(BF16)

    def cand_cot(k, part):
        r0 = (2 * k + part) * w
        return nt(cg, wcx[r0 : r0 + w])

    c2, c4 = cand_cot(2, 1), cand_cot(4, 1)
    c2b, c4b = c2.astype(BF16), c4.astype(BF16)
    rims[4].start(jnp.concatenate([nn(atf[nodes:], c2b), nn(atr[nodes:], c4b)], 1))
    f1 = cand_cot(1, 1) + 2.0 * nn(atf[:nodes], c2b)
    f3 = cand_cot(3, 1) + 2.0 * nn(atr[:nodes], c4b)
    rest_h = cand_cot(0, 1) - c2 - c4
    f1b, f3b = f1.astype(BF16), f3.astype(BF16)
    sent = nn(atf[nodes:], f1b) + nn(atr[nodes:], f3b)
    rest_h += nn(atf[:nodes], f1b) + nn(atr[:nodes], f3b)

    low = lax.broadcasted_iota(jnp.int32, (half, w), 1) < half

    def fold(m):
        t = jnp.where(low[:1] if m[0].shape[0] == 1 else low, m[0], m[1])
        return t + pltpu.roll(t, half, 1)

    def colsum(v):
        s = jnp.sum(v.astype(F32), 0, keepdims=True)
        s = jnp.broadcast_to(s, (8, w))
        return s + pltpu.roll(s, half, 1)

    def both(mx, mh):
        return [fold((mx[:half], mx[half:])), fold((mh[:half], mh[half:]))]

    for k in range(KS):
        sx = sup_ref[:, 2 * k * w : (2 * k + 1) * w]
        sh = sup_ref[:, (2 * k + 1) * w : (2 * k + 2) * w]
        th = cand_ref[:, k * w : (k + 1) * w]
        yc = both(tn(sx, cg), tn(th, cg))
        yu = both(tn(sx, gu), tn(sh, gu))
        for part in range(2):
            r0 = k * CH + part * half
            sum1.stage[r0 : r0 + half] = jnp.where(low, yc[part], yu[part])
    used = KS * CH
    sum1.stage[used : used + 8] = jnp.where(low8, colsum(cg), colsum(gu))
    if sum1.stage.shape[0] > used + 8:
        sum1.stage[used + 8 :] = jnp.zeros((sum1.stage.shape[0] - used - 8, w), F32)
    sum1.phase1()

    rim = rims[4].arrived()
    sent += 2.0 * (nn(af_back, rim[:, :w]) + nn(ar_back, rim[:, w:]))
    rims[5].start(sent)
    back = (2.0 * nn(sel_t, rim)).astype(BF16)
    rest_h += nn(atf[:nodes], back[:, :w]) + nn(atr[:nodes], back[:, w:])
    for k in range(KS):
        rows = slice(2 * k * w, 2 * (k + 1) * w)
        part = nt(gu, wgx[rows, w:])
        g_ref[:, 2 * k * w : (2 * k + 1) * w] = part[:, :w] + cand_cot(k, 0)
        g_ref[:, (2 * k + 1) * w : 2 * (k + 1) * w] = part[:, w:]
    sum1.phase2()
    gated_grad = rest_h + nn(sel_t, rims[5].arrived())

    gr = (gated_grad * hf * reset * (1.0 - reset)).astype(BF16)

    def gate_cot(k):
        cols = slice(2 * k * w, 2 * (k + 1) * w)
        return g_ref[:, cols] + nt(gr, wgx[cols, :w])

    g2, g4 = gate_cot(2), gate_cot(4)
    g2b, g4b = g2.astype(BF16), g4.astype(BF16)
    rims[6].start(jnp.concatenate([nn(atf[nodes:], g2b), nn(atr[nodes:], g4b)], 1))
    f1 = gate_cot(1) + 2.0 * nn(atf[:nodes], g2b)
    f3 = gate_cot(3) + 2.0 * nn(atr[:nodes], g4b)
    rest_all = gate_cot(0) - g2 - g4
    f1b, f3b = f1.astype(BF16), f3.astype(BF16)
    sent = nn(atf[nodes:], f1b) + nn(atr[nodes:], f3b)
    folded = []
    for k in range(KS):
        sx = sup_ref[:, 2 * k * w : (2 * k + 1) * w]
        sh = sup_ref[:, (2 * k + 1) * w : (2 * k + 2) * w]
        folded += both(tn(sx, gr), tn(sh, gr))
    for m in range(KS):
        sum2.stage[m * half : (m + 1) * half] = jnp.where(low, folded[m], folded[m + KS])
    used = KS * half
    sum2.stage[used : used + 8] = colsum(gr)
    if sum2.stage.shape[0] > used + 8:
        sum2.stage[used + 8 :] = jnp.zeros((sum2.stage.shape[0] - used - 8, w), F32)
    sum2.phase1()
    sum1.phase3()

    rim = rims[6].arrived()
    sent += 2.0 * (nn(af_back, rim[:, : 2 * w]) + nn(ar_back, rim[:, 2 * w :]))
    rims[7].start(sent)
    sum1.phase4()
    back = (2.0 * nn(sel_t, rim)).astype(BF16)
    rest_all += nn(atf[:nodes], f1b) + nn(atr[:nodes], f3b)
    rest_all += nn(atf[:nodes], back[:, : 2 * w]) + nn(atr[:nodes], back[:, 2 * w :])
    sum2.phase2()
    sum1.phase5()
    used = KS * CH
    total1 = sum1.out[...].reshape(-1, w)[: used + 8].astype(F32) * scale
    cand_grad_ref[...] = total1[:used].T[:half]
    cand_bias_grad_ref[...] = total1[used : used + 1, :half]
    rest_all += nn(sel_t, rims[7].arrived())
    in_grad_ref[...] = rest_all[:, :w]
    state_grad_ref[...] = cot * update + gated_grad * reset + rest_all[:, w:]
    sum2.phase3()
    used2 = used // 2
    total2 = sum2.out[...].reshape(-1, w)[: used2 + 8].astype(F32) * scale
    gate_bias_grad_ref[...] = jnp.where(low8, total2[used2:], total1[used:])[:1]
    wide = jnp.broadcast_to(low[:1], (used2, w))
    gate_grad_ref[:used2] = jnp.where(wide, total2[:used2], total1[:used2])
    gate_grad_ref[used2:] = jnp.where(wide, pltpu.roll(total2[:used2], half, 1), total1[used2:used])
    for rim in rims:
        rim.finish()
    sum1.finish()
    sum2.finish()


def on_device(
    layer_input,
    hidden_state,
    hidden_grad,
    gate_weight,
    gate_bias,
    candidate_weight,
    candidate_bias,
    forward_tiles,
    forward_columns,
    reverse_tiles,
    reverse_columns,
    send_rows,
    send_count,
):
    ng, nb = lax.axis_size("graph"), lax.axis_size("batch")
    nodes, w = layer_input.shape
    set_count, slot = send_rows.shape[1:]
    halo = set_count * slot
    r1 = chunk_rows(KS * CH + 8, ng * nb)
    r2 = chunk_rows(KS * CH // 2 + 8, ng * nb)
    widths = (2 * w, 4 * w, w, 2 * w, 2 * w, w, 4 * w, 2 * w)
    scratch = [
        pltpu.VMEM((KS * 2 * w, 2 * w), BF16),
        pltpu.VMEM((KS * 2 * w, w), BF16),
        pltpu.VMEM((2 * nodes, nodes + halo), BF16),
        pltpu.VMEM((nodes + halo, 2 * nodes), BF16),
        pltpu.VMEM((nodes, KS * 2 * w), BF16),
        pltpu.VMEM((nodes, KS * w), BF16),
        pltpu.VMEM((nodes, KS * 2 * w), F32),
    ]
    dma = lambda count: pltpu.SemaphoreType.DMA((count,))
    for width in widths:
        scratch += [
            pltpu.VMEM((halo, width), BF16),
            pltpu.VMEM((halo, width), BF16),
            dma(set_count),
            dma(set_count),
        ]
    n = nb * ng
    scratch += [
        pltpu.VMEM((n * r1, w), F32),
        pltpu.VMEM((nb, ng * r1, w), BF16),
        pltpu.VMEM((nb, ng * r1, w), BF16),
        pltpu.VMEM((ng, r1, w), BF16),
        pltpu.VMEM((ng, r1, w), BF16),
        pltpu.VMEM((ng, r1, w), BF16),
        pltpu.VMEM((nb, ng, r1, w), BF16),
    ]
    scratch += [dma(count) for count in (nb, nb, ng, ng, ng, ng, nb, nb)]
    scratch += [
        pltpu.VMEM((n * r2, w), F32),
        pltpu.VMEM((n, r2, w), BF16),
        pltpu.VMEM((n, r2, w), BF16),
        pltpu.VMEM((n, r2, w), BF16),
    ]
    scratch += [dma(n)] * 4
    vmem = pl.BlockSpec(memory_space=pltpu.VMEM)
    smem = pl.BlockSpec(memory_space=pltpu.SMEM)
    scale = 1.0 / math.sqrt(nodes * ng * (w // HID) * nb)
    grads = pl.pallas_call(
        functools.partial(step_kernel, ng, nb, scale),
        name="gru_backward",
        out_shape=(
            jax.ShapeDtypeStruct((nodes, w), F32),
            jax.ShapeDtypeStruct((nodes, w), F32),
            jax.ShapeDtypeStruct((KS * CH, 2 * HID), F32),
            jax.ShapeDtypeStruct((1, 2 * HID), F32),
            jax.ShapeDtypeStruct((HID, KS * CH), F32),
            jax.ShapeDtypeStruct((1, HID), F32),
        ),
        in_specs=[vmem] * 8 + [smem, vmem, smem, vmem, smem],
        out_specs=(vmem,) * 6,
        scratch_shapes=scratch,
        compiler_params=pltpu.CompilerParams(
            collective_id=0, has_side_effects=True, vmem_limit_bytes=32 * 1024 * 1024
        ),
    )(
        layer_input,
        hidden_state,
        hidden_grad,
        gate_weight,
        gate_bias.reshape(1, 2 * HID),
        candidate_weight.T,
        candidate_bias.reshape(1, HID),
        forward_tiles,
        forward_columns,
        reverse_tiles,
        reverse_columns,
        send_rows,
        send_count,
    )
    input_grad, state_grad, gate_grad, gate_bias_grad, cand_grad, cand_bias_grad = grads
    return (
        input_grad,
        state_grad,
        gate_grad,
        gate_bias_grad.reshape(2 * HID),
        cand_grad.T,
        cand_bias_grad.reshape(HID),
    )


def solution(mesh):
    placed = (
        P("graph", "batch"),
        P("graph", "batch"),
        P("graph", "batch"),
        P(),
        P(),
        P(),
        P(),
        P("graph", None, None, None),
        P("graph", None),
        P("graph", None, None, None),
        P("graph", None),
        P("graph", None, None),
        P("graph", None),
    )
    return jax.shard_map(
        on_device,
        mesh=mesh,
        in_specs=placed,
        out_specs=(P("graph", "batch"), P("graph", "batch"), P(), P(), P(), P()),
        check_vma=False,
    )
```

```python
import functools
import math

import jax
import jax.numpy as jnp
from jax import lax
from jax.experimental import pallas as pl
from jax.experimental.pallas import tpu as pltpu
from jax.sharding import PartitionSpec as P

HID = 64
KS = 5
CH = 128
MESH = pl.DeviceIdType.MESH
F32 = jnp.float32
BF16 = jnp.bfloat16


def rim_offsets(set_count):
    return [(number // 2 + 1) * (1 - 2 * (number % 2)) for number in range(set_count)]


def chunk_rows(rows, parts):
    return -(-(-(-rows // parts)) // 8) * 8


def nn(a, b):
    return lax.dot_general(a, b, (((1,), (0,)), ((), ())), preferred_element_type=F32)


def nt(a, b):
    return lax.dot_general(a, b, (((1,), (1,)), ((), ())), preferred_element_type=F32)


def tn(a, b):
    return lax.dot_general(a, b, (((0,), (0,)), ((), ())), preferred_element_type=F32)


class Rim:
    def __init__(self, n, me, offsets, sign, refs):
        self.n, self.me, self.sign = n, me, sign
        self.offsets = offsets
        self.out, self.into, self.send_sem, self.recv_sem = refs
        self.slot = self.out.shape[0] // len(offsets)

    def copy(self, j, device):
        rows = pl.ds(j * self.slot, self.slot)
        return pltpu.make_async_remote_copy(
            src_ref=self.out.at[rows],
            dst_ref=self.into.at[rows],
            send_sem=self.send_sem.at[j],
            recv_sem=self.recv_sem.at[j],
            device_id={"graph": device},
            device_id_type=MESH,
        )

    def each(self, sign, act):
        for j, offset in enumerate(self.offsets):
            other = self.me + sign * offset
            pl.when((other >= 0) & (other < self.n))(functools.partial(act, j, other))

    def start(self, value):
        self.out[...] = value.astype(BF16)
        self.each(self.sign, lambda j, other: self.copy(j, other).start())

    def arrived(self):
        self.each(-self.sign, lambda j, other: self.copy(j, other).wait_recv())
        return self.into[...]

    def finish(self):
        self.each(self.sign, lambda j, other: self.copy(j, other).wait_send())


class Total:
    def __init__(self, nb, ng, mb, mg, refs):
        self.nb, self.ng, self.mb, self.mg = nb, ng, mb, mg
        self.stage, self.mine, self.got, self.part, self.heard, self.slab, self.out = refs[:7]
        self.sems = refs[7:]
        self.started = []

    def copy(self, phase, axis, count, me, src, dst):
        send_sem, recv_sem = self.sems[2 * phase], self.sems[2 * phase + 1]
        for d in range(1, count):
            other = lax.rem(me + d, count)
            c = pltpu.make_async_remote_copy(
                src_ref=src(other),
                dst_ref=dst(d),
                send_sem=send_sem.at[d],
                recv_sem=recv_sem.at[d],
                device_id={axis: other},
                device_id_type=MESH,
            )
            c.start()
            self.started.append(c)
        return self.started[len(self.started) - (count - 1) :] if count > 1 else []

    def phase1(self):
        self.mine[...] = self.stage[...].reshape(self.mine.shape).astype(BF16)
        self.wait = self.copy(
            0, "batch", self.nb, self.mb, lambda o: self.mine.at[o], lambda d: self.got.at[d]
        )

    def phase2(self):
        for c in self.wait:
            c.wait_recv()
        total = self.mine[self.mb].astype(F32)
        for d in range(1, self.nb):
            total += self.got[d].astype(F32)
        self.part[...] = total.reshape(self.part.shape).astype(BF16)
        self.wait = self.copy(
            1, "graph", self.ng, self.mg, lambda o: self.part.at[o], lambda d: self.heard.at[d]
        )

    def phase3(self):
        for c in self.wait:
            c.wait_recv()
        total = self.part[self.mg].astype(F32)
        for d in range(1, self.ng):
            total += self.heard[d].astype(F32)
        self.slab[self.mg] = total.astype(BF16)
        self.wait = self.copy(
            2,
            "graph",
            self.ng,
            self.mg,
            lambda o: self.slab.at[self.mg],
            lambda d: self.slab.at[self.mg],
        )

    def phase4(self):
        for c in self.wait:
            c.wait_recv()
        self.wait = self.copy(
            3, "batch", self.nb, self.mb, lambda o: self.slab, lambda d: self.out.at[self.mb]
        )
        self.out[self.mb] = self.slab[...]

    def phase5(self):
        for c in self.wait:
            c.wait_recv()

    def finish(self):
        for c in self.started:
            c.wait_send()


class Direct:
    def __init__(self, nb, ng, mb, mg, refs):
        self.n, self.ng = nb * ng, ng
        self.me = mb * ng + mg
        self.stage, self.mine, self.got, self.out = refs[:4]
        self.sems = refs[4:]
        self.started = []

    def copy(self, phase, src, dst):
        send_sem, recv_sem = self.sems[2 * phase], self.sems[2 * phase + 1]
        self.wait = []
        for d in range(1, self.n):
            other = lax.rem(self.me + d, self.n)
            c = pltpu.make_async_remote_copy(
                src_ref=src(other),
                dst_ref=dst(d),
                send_sem=send_sem.at[d],
                recv_sem=recv_sem.at[d],
                device_id={"graph": lax.rem(other, self.ng), "batch": lax.div(other, self.ng)},
                device_id_type=MESH,
            )
            c.start()
            self.wait.append(c)
        self.started += self.wait

    def phase1(self):
        self.mine[...] = self.stage[...].reshape(self.mine.shape).astype(BF16)
        self.copy(0, lambda o: self.mine.at[o], lambda d: self.got.at[d])

    def phase2(self):
        for c in self.wait:
            c.wait_recv()
        total = self.mine[self.me].astype(F32)
        for d in range(1, self.n):
            total += self.got[d].astype(F32)
        self.out[self.me] = total.astype(BF16)
        self.copy(1, lambda o: self.out.at[self.me], lambda d: self.out.at[self.me])

    def phase3(self):
        for c in self.wait:
            c.wait_recv()

    def finish(self):
        for c in self.started:
            c.wait_send()


def step_kernel(
    ng,
    nb,
    scale,
    x_hbm,
    h_hbm,
    cot_hbm,
    wg_hbm,
    gate_bias_hbm,
    wc_hbm,
    cand_bias_hbm,
    ft_hbm,
    fc_ref,
    rt_hbm,
    rc_ref,
    list_ref,
    count_ref,
    in_grad_ref,
    state_grad_ref,
    gate_grad_ref,
    gate_bias_grad_ref,
    cand_grad_ref,
    cand_bias_grad_ref,
    *scratch,
):
    set_count, slot = list_ref.shape[1:]
    fetch_sem = scratch[-1]
    sources = (x_hbm, h_hbm, ft_hbm, rt_hbm, wg_hbm, wc_hbm, gate_bias_hbm, cand_bias_hbm, cot_hbm)
    held = scratch[-10:-1]
    scratch = scratch[:-10]
    fetches = [
        pltpu.make_async_copy(source, target, fetch_sem.at[number])
        for number, (source, target) in enumerate(zip(sources, held))
    ]
    for fetch in fetches:
        fetch.start()
    x_ref, h_ref, ft_ref, rt_ref, wg_ref, wc_ref, gate_bias_ref, cand_bias_ref, cot_ref = held
    mg, mb = lax.axis_index("graph"), lax.axis_index("batch")
    nodes = x_ref.shape[0]
    w = x_ref.shape[1]
    half = w // 2
    tile = ft_ref.shape[2]
    rows_i, tpr = ft_ref.shape[:2]
    halo = set_count * slot
    blocks = (nodes + halo) // tile
    offsets = rim_offsets(set_count)
    wgx, wcx, a_ref, at_ref, sup_ref, cand_ref, g_ref = scratch[:7]
    rest = list(scratch[7:])
    signs = (1, 1, 1, 1, -1, -1, -1, -1)
    rims = [Rim(ng, mg, offsets, signs[e], rest[4 * e : 4 * e + 4]) for e in range(8)]
    rest = rest[32:]
    sum1 = Total(nb, ng, mb, mg, rest[:15])
    sum2 = Direct(nb, ng, mb, mg, rest[15:])

    for rim in rims:
        rim.into[...] = jnp.zeros(rim.into.shape, BF16)
    barrier = pltpu.get_barrier_semaphore()
    n, me = nb * ng, mb * ng + mg
    for d in range(1, n):
        other = lax.rem(me + d, n)
        pl.semaphore_signal(
            barrier,
            inc=1,
            device_id={"graph": lax.rem(other, ng), "batch": lax.div(other, ng)},
            device_id_type=MESH,
        )

    ids = lax.broadcasted_iota(jnp.int32, (1, slot), 1)
    listed = jnp.concatenate(
        [jnp.where(ids < count_ref[0, j], list_ref[0, j : j + 1, :], -1) for j in range(set_count)],
        1,
    )
    sel_f = jnp.where(
        lax.broadcasted_iota(jnp.int32, (nodes, halo), 0)
        == jnp.broadcast_to(listed, (nodes, halo)),
        1.0,
        0.0,
    )
    sel_t = sel_f.astype(BF16)
    sel = sel_f.T.astype(BF16)

    for fetch in fetches[:2]:
        fetch.wait()
    x = x_ref[...]
    h = h_ref[...]
    sup_ref[:, :w] = x
    sup_ref[:, w : 2 * w] = h
    values = sup_ref[:, : 2 * w]
    first = nn(sel, values)

    for fetch in fetches[2:4]:
        fetch.wait()
    for side, (tiles, cols) in enumerate(((ft_ref, fc_ref), (rt_ref, rc_ref))):
        for i in range(rows_i):
            for b in range(blocks):
                acc = None
                for t in range(tpr):
                    keep = (cols[i, t] == b).astype(F32)
                    term = tiles[i, t].astype(F32) * keep
                    acc = term if acc is None else acc + term
                r0 = side * nodes + i * tile
                a_ref[r0 : r0 + tile, b * tile : (b + 1) * tile] = acc.astype(BF16)
                at_ref[b * tile : (b + 1) * tile, r0 : r0 + tile] = acc.T.astype(BF16)

    pl.semaphore_wait(barrier, n - 1)
    rims[0].start(first)

    own = a_ref[:, :nodes]
    af_sent = nn(sel, a_ref[:nodes, :]).astype(BF16)
    ar_sent = nn(sel, a_ref[nodes:, :]).astype(BF16)
    sent13 = [nn(m[:, :nodes], values) for m in (af_sent, ar_sent)]
    local13 = nn(own, values)

    for fetch in fetches[4:]:
        fetch.wait()

    def widen(weight, columns, outs):
        pieces = []
        for k in range(KS):
            low = weight[k * CH : k * CH + half]
            high = weight[k * CH + half : (k + 1) * CH]
            pieces += [low, low, high, high]
        tall = jnp.concatenate(pieces, 0)
        i = lax.broadcasted_iota(jnp.int32, (columns, outs), 0)
        j = lax.broadcasted_iota(jnp.int32, (columns, outs), 1)
        pick = jnp.where(i == (j // w) * half + j % half, 1.0, 0.0).astype(BF16)
        wide = nn(tall, pick)
        i = lax.broadcasted_iota(jnp.int32, wide.shape, 0)
        j = lax.broadcasted_iota(jnp.int32, wide.shape, 1)
        return jnp.where((i // half) % 2 == (j // half) % 2, wide, 0.0).astype(BF16)

    wgx[...] = widen(wg_ref[...], 2 * HID, 2 * w)
    wcx[...] = widen(wc_ref[...].astype(F32).T.astype(BF16), HID, w)
    atf, atr = at_ref[:, :nodes], at_ref[:, nodes:]
    af_back = nn(atf[nodes:], sel_t).astype(BF16)
    ar_back = nn(atr[nodes:], sel_t).astype(BF16)

    gate_bias = jnp.broadcast_to(gate_bias_ref[...], (8, w))
    turned = pltpu.roll(gate_bias, half, 1)
    low8 = lax.broadcasted_iota(jnp.int32, (8, w), 1) < half
    reset_bias = jnp.where(low8, gate_bias, turned)[:1]
    update_bias = jnp.where(low8, turned, gate_bias)[:1]
    cand_bias = jnp.concatenate([cand_bias_ref[...]] * 2, 1)

    rim = rims[0].arrived()
    sent = [m + nn(a[:, nodes:], rim) for m, a in zip(sent13, (af_sent, ar_sent))]
    rims[1].start(jnp.concatenate(sent, 1))
    s13 = local13 + nn(a_ref[:, nodes:], rim)
    s1 = s13[:nodes].astype(BF16)
    s3 = s13[nodes:].astype(BF16)
    sup_ref[:, 2 * w : 4 * w] = s1
    sup_ref[:, 6 * w : 8 * w] = s3
    base = values.astype(F32)
    l2 = nn(a_ref[:nodes, :nodes], s1)
    l4 = nn(a_ref[nodes:, :nodes], s3)
    pre = nn(values, wgx[: 2 * w]) + nn(s1, wgx[2 * w : 4 * w]) + nn(s3, wgx[6 * w : 8 * w])
    rim = rims[1].arrived()
    l2 += nn(a_ref[:nodes, nodes:], rim[:, : 2 * w])
    l4 += nn(a_ref[nodes:, nodes:], rim[:, 2 * w :])
    s2 = (2.0 * l2 - base).astype(BF16)
    s4 = (2.0 * l4 - base).astype(BF16)
    sup_ref[:, 4 * w : 6 * w] = s2
    sup_ref[:, 8 * w :] = s4
    pre += nn(s2, wgx[4 * w : 6 * w]) + nn(s4, wgx[8 * w :])
    hf = h.astype(F32)
    reset = jax.nn.sigmoid(pre[:, :w] + reset_bias)
    update = jax.nn.sigmoid(pre[:, w:] + update_bias)

    gated = (reset * hf).astype(BF16)
    rims[2].start(nn(sel, gated))
    cand_ref[:, :w] = gated
    sent13 = [nn(m[:, :nodes], gated) for m in (af_sent, ar_sent)]
    l13 = nn(own, gated)
    cpre = nn(gated, wcx[w : 2 * w])
    for k in range(KS):
        cpre += nn(sup_ref[:, 2 * k * w : (2 * k + 1) * w], wcx[2 * k * w : (2 * k + 1) * w])
    rim = rims[2].arrived()
    sent = [m + nn(a[:, nodes:], rim) for m, a in zip(sent13, (af_sent, ar_sent))]
    rims[3].start(jnp.concatenate(sent, 1))
    l13 += nn(a_ref[:, nodes:], rim)
    t1 = l13[:nodes].astype(BF16)
    t3 = l13[nodes:].astype(BF16)
    cand_ref[:, w : 2 * w] = t1
    cand_ref[:, 3 * w : 4 * w] = t3
    l2 = nn(a_ref[:nodes, :nodes], t1)
    l4 = nn(a_ref[nodes:, :nodes], t3)
    cpre += nn(t1, wcx[3 * w : 4 * w]) + nn(t3, wcx[7 * w : 8 * w])
    rim = rims[3].arrived()
    l2 += nn(a_ref[:nodes, nodes:], rim[:, :w])
    l4 += nn(a_ref[nodes:, nodes:], rim[:, w:])
    gatedf = gated.astype(F32)
    t2 = (2.0 * l2 - gatedf).astype(BF16)
    t4 = (2.0 * l4 - gatedf).astype(BF16)
    cand_ref[:, 2 * w : 3 * w] = t2
    cand_ref[:, 4 * w :] = t4
    cpre += nn(t2, wcx[5 * w : 6 * w]) + nn(t4, wcx[9 * w :])
    cand = jnp.tanh(cpre + cand_bias)

    cot = cot_ref[...].astype(F32)
    update_grad = cot * (hf - cand)
    cg = (cot * (1.0 - update) * (1.0 - cand * cand)).astype(BF16)
    gu = (update_grad * update * (1.0 - update)).astype(BF16)

    def cand_cot(k, part):
        r0 = (2 * k + part) * w
        return nt(cg, wcx[r0 : r0 + w])

    c2, c4 = cand_cot(2, 1), cand_cot(4, 1)
    c2b, c4b = c2.astype(BF16), c4.astype(BF16)
    rims[4].start(jnp.concatenate([nn(atf[nodes:], c2b), nn(atr[nodes:], c4b)], 1))
    f1 = cand_cot(1, 1) + 2.0 * nn(atf[:nodes], c2b)
    f3 = cand_cot(3, 1) + 2.0 * nn(atr[:nodes], c4b)
    rest_h = cand_cot(0, 1) - c2 - c4
    f1b, f3b = f1.astype(BF16), f3.astype(BF16)
    sent = nn(atf[nodes:], f1b) + nn(atr[nodes:], f3b)
    rest_h += nn(atf[:nodes], f1b) + nn(atr[:nodes], f3b)

    low = lax.broadcasted_iota(jnp.int32, (half, w), 1) < half

    def fold(m):
        t = jnp.where(low[:1] if m[0].shape[0] == 1 else low, m[0], m[1])
        return t + pltpu.roll(t, half, 1)

    def colsum(v):
        s = jnp.sum(v.astype(F32), 0, keepdims=True)
        s = jnp.broadcast_to(s, (8, w))
        return s + pltpu.roll(s, half, 1)

    def both(mx, mh):
        return [fold((mx[:half], mx[half:])), fold((mh[:half], mh[half:]))]

    for k in range(KS):
        sx = sup_ref[:, 2 * k * w : (2 * k + 1) * w]
        sh = sup_ref[:, (2 * k + 1) * w : (2 * k + 2) * w]
        th = cand_ref[:, k * w : (k + 1) * w]
        yc = both(tn(sx, cg), tn(th, cg))
        yu = both(tn(sx, gu), tn(sh, gu))
        for part in range(2):
            r0 = k * CH + part * half
            sum1.stage[r0 : r0 + half] = jnp.where(low, yc[part], yu[part])
    used = KS * CH
    sum1.stage[used : used + 8] = jnp.where(low8, colsum(cg), colsum(gu))
    if sum1.stage.shape[0] > used + 8:
        sum1.stage[used + 8 :] = jnp.zeros((sum1.stage.shape[0] - used - 8, w), F32)
    sum1.phase1()

    rim = rims[4].arrived()
    sent += 2.0 * (nn(af_back, rim[:, :w]) + nn(ar_back, rim[:, w:]))
    rims[5].start(sent)
    back = (2.0 * nn(sel_t, rim)).astype(BF16)
    rest_h += nn(atf[:nodes], back[:, :w]) + nn(atr[:nodes], back[:, w:])
    for k in range(KS):
        rows = slice(2 * k * w, 2 * (k + 1) * w)
        part = nt(gu, wgx[rows, w:])
        g_ref[:, 2 * k * w : (2 * k + 1) * w] = part[:, :w] + cand_cot(k, 0)
        g_ref[:, (2 * k + 1) * w : 2 * (k + 1) * w] = part[:, w:]
    sum1.phase2()
    gated_grad = rest_h + nn(sel_t, rims[5].arrived())

    gr = (gated_grad * hf * reset * (1.0 - reset)).astype(BF16)

    def gate_cot(k):
        cols = slice(2 * k * w, 2 * (k + 1) * w)
        return g_ref[:, cols] + nt(gr, wgx[cols, :w])

    g2, g4 = gate_cot(2), gate_cot(4)
    g2b, g4b = g2.astype(BF16), g4.astype(BF16)
    rims[6].start(jnp.concatenate([nn(atf[nodes:], g2b), nn(atr[nodes:], g4b)], 1))
    f1 = gate_cot(1) + 2.0 * nn(atf[:nodes], g2b)
    f3 = gate_cot(3) + 2.0 * nn(atr[:nodes], g4b)
    rest_all = gate_cot(0) - g2 - g4
    f1b, f3b = f1.astype(BF16), f3.astype(BF16)
    sent = nn(atf[nodes:], f1b) + nn(atr[nodes:], f3b)
    folded = []
    for k in range(KS):
        sx = sup_ref[:, 2 * k * w : (2 * k + 1) * w]
        sh = sup_ref[:, (2 * k + 1) * w : (2 * k + 2) * w]
        folded += both(tn(sx, gr), tn(sh, gr))
    for m in range(KS):
        sum2.stage[m * half : (m + 1) * half] = jnp.where(low, folded[m], folded[m + KS])
    used = KS * half
    sum2.stage[used : used + 8] = colsum(gr)
    if sum2.stage.shape[0] > used + 8:
        sum2.stage[used + 8 :] = jnp.zeros((sum2.stage.shape[0] - used - 8, w), F32)
    sum2.phase1()
    sum1.phase3()

    rim = rims[6].arrived()
    sent += 2.0 * (nn(af_back, rim[:, : 2 * w]) + nn(ar_back, rim[:, 2 * w :]))
    rims[7].start(sent)
    sum1.phase4()
    back = (2.0 * nn(sel_t, rim)).astype(BF16)
    rest_all += nn(atf[:nodes], f1b) + nn(atr[:nodes], f3b)
    rest_all += nn(atf[:nodes], back[:, : 2 * w]) + nn(atr[:nodes], back[:, 2 * w :])
    sum2.phase2()
    sum1.phase5()
    used = KS * CH
    total1 = sum1.out[...].reshape(-1, w)[: used + 8].astype(F32) * scale
    cand_grad_ref[...] = total1[:used].T[:half]
    cand_bias_grad_ref[...] = total1[used : used + 1, :half]
    rest_all += nn(sel_t, rims[7].arrived())
    in_grad_ref[...] = rest_all[:, :w]
    state_grad_ref[...] = cot * update + gated_grad * reset + rest_all[:, w:]
    sum2.phase3()
    used2 = used // 2
    total2 = sum2.out[...].reshape(-1, w)[: used2 + 8].astype(F32) * scale
    gate_bias_grad_ref[...] = jnp.where(low8, total2[used2:], total1[used:])[:1]
    wide = jnp.broadcast_to(low[:1], (used2, w))
    gate_grad_ref[:used2] = jnp.where(wide, total2[:used2], total1[:used2])
    gate_grad_ref[used2:] = jnp.where(wide, pltpu.roll(total2[:used2], half, 1), total1[used2:used])
    for rim in rims:
        rim.finish()
    sum1.finish()
    sum2.finish()


def deliver_kernel(count, *refs):
    sources, targets, held = refs[:count], refs[count : 2 * count], refs[2 * count : 3 * count]
    in_sem, out_sem = refs[3 * count :]
    loads = [
        pltpu.make_async_copy(sources[i], held[i], in_sem.at[i]) for i in range(count)
    ]
    stores = [
        pltpu.make_async_copy(held[i], targets[i], out_sem.at[i]) for i in range(count)
    ]
    for load in loads:
        load.start()
    for load, store in zip(loads, stores):
        load.wait()
        store.start()
    for store in stores:
        store.wait()


def deliver(arrays):
    count = len(arrays)
    shapes = [(a.shape, a.dtype) for a in arrays]
    hbm = pl.BlockSpec(memory_space=pltpu.HBM)
    return pl.pallas_call(
        functools.partial(deliver_kernel, count),
        name="deliver",
        out_shape=tuple(jax.ShapeDtypeStruct(*shape) for shape in shapes),
        in_specs=[hbm] * count,
        out_specs=(hbm,) * count,
        scratch_shapes=[pltpu.VMEM(*shape) for shape in shapes]
        + [pltpu.SemaphoreType.DMA((count,))] * 2,
        compiler_params=pltpu.CompilerParams(vmem_limit_bytes=60 * 1024 * 1024),
    )(*arrays)


def on_device(
    layer_input,
    hidden_state,
    hidden_grad,
    gate_weight,
    gate_bias,
    candidate_weight,
    candidate_bias,
    forward_tiles,
    forward_columns,
    reverse_tiles,
    reverse_columns,
    send_rows,
    send_count,
):
    ng, nb = lax.axis_size("graph"), lax.axis_size("batch")
    nodes, w = layer_input.shape
    set_count, slot = send_rows.shape[1:]
    halo = set_count * slot
    r1 = chunk_rows(KS * CH + 8, ng * nb)
    r2 = chunk_rows(KS * CH // 2 + 8, ng * nb)
    widths = (2 * w, 4 * w, w, 2 * w, 2 * w, w, 4 * w, 2 * w)
    scratch = [
        pltpu.VMEM((KS * 2 * w, 2 * w), BF16),
        pltpu.VMEM((KS * 2 * w, w), BF16),
        pltpu.VMEM((2 * nodes, nodes + halo), BF16),
        pltpu.VMEM((nodes + halo, 2 * nodes), BF16),
        pltpu.VMEM((nodes, KS * 2 * w), BF16),
        pltpu.VMEM((nodes, KS * w), BF16),
        pltpu.VMEM((nodes, KS * 2 * w), F32),
    ]
    dma = lambda count: pltpu.SemaphoreType.DMA((count,))
    for width in widths:
        scratch += [
            pltpu.VMEM((halo, width), BF16),
            pltpu.VMEM((halo, width), BF16),
            dma(set_count),
            dma(set_count),
        ]
    n = nb * ng
    scratch += [
        pltpu.VMEM((n * r1, w), F32),
        pltpu.VMEM((nb, ng * r1, w), BF16),
        pltpu.VMEM((nb, ng * r1, w), BF16),
        pltpu.VMEM((ng, r1, w), BF16),
        pltpu.VMEM((ng, r1, w), BF16),
        pltpu.VMEM((ng, r1, w), BF16),
        pltpu.VMEM((nb, ng, r1, w), BF16),
    ]
    scratch += [dma(count) for count in (nb, nb, ng, ng, ng, ng, nb, nb)]
    scratch += [
        pltpu.VMEM((n * r2, w), F32),
        pltpu.VMEM((n, r2, w), BF16),
        pltpu.VMEM((n, r2, w), BF16),
        pltpu.VMEM((n, r2, w), BF16),
    ]
    scratch += [dma(n)] * 4
    fetched = (
        layer_input,
        hidden_state,
        forward_tiles,
        reverse_tiles,
        gate_weight,
        candidate_weight.T,
        gate_bias.reshape(1, 2 * HID),
        candidate_bias.reshape(1, HID),
        hidden_grad,
    )
    scratch += [pltpu.VMEM(a.shape, a.dtype) for a in fetched] + [dma(len(fetched))]
    vmem = pl.BlockSpec(memory_space=pltpu.VMEM)
    hbm = pl.BlockSpec(memory_space=pltpu.HBM)
    smem = pl.BlockSpec(memory_space=pltpu.SMEM)
    scale = 1.0 / math.sqrt(nodes * ng * (w // HID) * nb)
    grads = pl.pallas_call(
        functools.partial(step_kernel, ng, nb, scale),
        name="gru_backward",
        out_shape=(
            jax.ShapeDtypeStruct((nodes, w), F32),
            jax.ShapeDtypeStruct((nodes, w), F32),
            jax.ShapeDtypeStruct((KS * CH, 2 * HID), F32),
            jax.ShapeDtypeStruct((1, 2 * HID), F32),
            jax.ShapeDtypeStruct((HID, KS * CH), F32),
            jax.ShapeDtypeStruct((1, HID), F32),
        ),
        in_specs=[hbm] * 8 + [smem, hbm, smem, vmem, smem],
        out_specs=(vmem,) * 6,
        scratch_shapes=scratch,
        compiler_params=pltpu.CompilerParams(
            collective_id=0, has_side_effects=True, vmem_limit_bytes=60 * 1024 * 1024
        ),
    )(
        layer_input,
        hidden_state,
        hidden_grad,
        gate_weight,
        gate_bias.reshape(1, 2 * HID),
        candidate_weight.T,
        candidate_bias.reshape(1, HID),
        forward_tiles,
        forward_columns,
        reverse_tiles,
        reverse_columns,
        send_rows,
        send_count,
    )
    input_grad, state_grad, gate_grad, gate_bias_grad, cand_grad, cand_bias_grad = deliver(grads)
    return (
        input_grad,
        state_grad,
        gate_grad,
        gate_bias_grad.reshape(2 * HID),
        cand_grad.T,
        cand_bias_grad.reshape(HID),
    )


def solution(mesh):
    placed = (
        P("graph", "batch"),
        P("graph", "batch"),
        P("graph", "batch"),
        P(),
        P(),
        P(),
        P(),
        P("graph", None, None, None),
        P("graph", None),
        P("graph", None, None, None),
        P("graph", None),
        P("graph", None, None),
        P("graph", None),
    )
    return jax.shard_map(
        on_device,
        mesh=mesh,
        in_specs=placed,
        out_specs=(P("graph", "batch"), P("graph", "batch"), P(), P(), P(), P()),
        check_vma=False,
    )
```

```python
import functools
import math

import jax
import jax.numpy as jnp
from jax import lax
from jax.experimental import pallas as pl
from jax.experimental.pallas import tpu as pltpu
from jax.sharding import PartitionSpec as P

HID = 64
KS = 5
CH = 128
MESH = pl.DeviceIdType.MESH
F32 = jnp.float32
BF16 = jnp.bfloat16


def rim_offsets(set_count):
    return [(number // 2 + 1) * (1 - 2 * (number % 2)) for number in range(set_count)]


def chunk_rows(rows, parts):
    return -(-(-(-rows // parts)) // 8) * 8


def nn(a, b):
    return lax.dot_general(a, b, (((1,), (0,)), ((), ())), preferred_element_type=F32)


def nt(a, b):
    return lax.dot_general(a, b, (((1,), (1,)), ((), ())), preferred_element_type=F32)


def tn(a, b):
    return lax.dot_general(a, b, (((0,), (0,)), ((), ())), preferred_element_type=F32)


class Rim:
    def __init__(self, n, me, offsets, sign, refs):
        self.n, self.me, self.sign = n, me, sign
        self.offsets = offsets
        self.out, self.into, self.send_sem, self.recv_sem = refs
        self.slot = self.out.shape[0] // len(offsets)

    def copy(self, j, device):
        rows = pl.ds(j * self.slot, self.slot)
        return pltpu.make_async_remote_copy(
            src_ref=self.out.at[rows],
            dst_ref=self.into.at[rows],
            send_sem=self.send_sem.at[j],
            recv_sem=self.recv_sem.at[j],
            device_id={"graph": device},
            device_id_type=MESH,
        )

    def each(self, sign, act):
        for j, offset in enumerate(self.offsets):
            other = self.me + sign * offset
            pl.when((other >= 0) & (other < self.n))(functools.partial(act, j, other))

    def start(self, value):
        self.out[...] = value.astype(BF16)
        self.each(self.sign, lambda j, other: self.copy(j, other).start())

    def arrived(self):
        self.each(-self.sign, lambda j, other: self.copy(j, other).wait_recv())
        return self.into[...]

    def finish(self):
        self.each(self.sign, lambda j, other: self.copy(j, other).wait_send())


class Direct:
    def __init__(self, nb, ng, mb, mg, refs):
        self.n, self.ng = nb * ng, ng
        self.me = mb * ng + mg
        self.stage, self.mine, self.got, self.out = refs[:4]
        self.sems = refs[4:]
        self.started = []

    def copy(self, phase, src, dst):
        send_sem, recv_sem = self.sems[2 * phase], self.sems[2 * phase + 1]
        self.wait = []
        for d in range(1, self.n):
            other = lax.rem(self.me + d, self.n)
            c = pltpu.make_async_remote_copy(
                src_ref=src(other),
                dst_ref=dst(d),
                send_sem=send_sem.at[d],
                recv_sem=recv_sem.at[d],
                device_id={"graph": lax.rem(other, self.ng), "batch": lax.div(other, self.ng)},
                device_id_type=MESH,
            )
            c.start()
            self.wait.append(c)
        self.started += self.wait

    def phase1(self):
        self.mine[...] = self.stage[...].reshape(self.mine.shape).astype(BF16)
        self.copy(0, lambda o: self.mine.at[o], lambda d: self.got.at[d])

    def phase2(self):
        for c in self.wait:
            c.wait_recv()
        total = self.mine[self.me].astype(F32)
        for d in range(1, self.n):
            total += self.got[d].astype(F32)
        self.out[self.me] = total.astype(BF16)
        self.copy(1, lambda o: self.out.at[self.me], lambda d: self.out.at[self.me])

    def phase3(self):
        for c in self.wait:
            c.wait_recv()

    def finish(self):
        for c in self.started:
            c.wait_send()


def step_kernel(
    ng,
    nb,
    scale,
    x_hbm,
    h_hbm,
    cot_hbm,
    wg_hbm,
    gate_bias_hbm,
    wc_hbm,
    cand_bias_hbm,
    ft_hbm,
    fc_ref,
    rt_hbm,
    rc_ref,
    list_ref,
    count_ref,
    in_grad_ref,
    state_grad_ref,
    gate_grad_ref,
    gate_bias_grad_ref,
    cand_grad_ref,
    cand_bias_grad_ref,
    *scratch,
):
    set_count, slot = list_ref.shape[1:]
    fetch_sem = scratch[-1]
    sources = (x_hbm, h_hbm, ft_hbm, rt_hbm, wg_hbm, wc_hbm, gate_bias_hbm, cand_bias_hbm, cot_hbm)
    held = scratch[-10:-1]
    scratch = scratch[:-10]
    fetches = [
        pltpu.make_async_copy(source, target, fetch_sem.at[number])
        for number, (source, target) in enumerate(zip(sources, held))
    ]
    for fetch in fetches:
        fetch.start()
    x_ref, h_ref, ft_ref, rt_ref, wg_ref, wc_ref, gate_bias_ref, cand_bias_ref, cot_ref = held
    mg, mb = lax.axis_index("graph"), lax.axis_index("batch")
    nodes = x_ref.shape[0]
    w = x_ref.shape[1]
    half = w // 2
    tile = ft_ref.shape[2]
    rows_i, tpr = ft_ref.shape[:2]
    halo = set_count * slot
    blocks = (nodes + halo) // tile
    offsets = rim_offsets(set_count)
    wgx, wcx, a_ref, at_ref, sup_ref, cand_ref, g_ref = scratch[:7]
    rest = list(scratch[7:])
    signs = (1, 1, 1, 1, -1, -1, -1, -1)
    rims = [Rim(ng, mg, offsets, signs[e], rest[4 * e : 4 * e + 4]) for e in range(8)]
    rest = rest[32:]
    sum1 = Direct(nb, ng, mb, mg, rest[:8])
    sum2 = Direct(nb, ng, mb, mg, rest[8:])

    for rim in rims:
        rim.into[...] = jnp.zeros(rim.into.shape, BF16)
    barrier = pltpu.get_barrier_semaphore()
    n, me = nb * ng, mb * ng + mg
    for d in range(1, n):
        other = lax.rem(me + d, n)
        pl.semaphore_signal(
            barrier,
            inc=1,
            device_id={"graph": lax.rem(other, ng), "batch": lax.div(other, ng)},
            device_id_type=MESH,
        )

    ids = lax.broadcasted_iota(jnp.int32, (1, slot), 1)
    listed = jnp.concatenate(
        [jnp.where(ids < count_ref[0, j], list_ref[0, j : j + 1, :], -1) for j in range(set_count)],
        1,
    )
    sel_f = jnp.where(
        lax.broadcasted_iota(jnp.int32, (nodes, halo), 0)
        == jnp.broadcast_to(listed, (nodes, halo)),
        1.0,
        0.0,
    )
    sel_t = sel_f.astype(BF16)
    sel = sel_f.T.astype(BF16)

    for fetch in fetches[:2]:
        fetch.wait()
    x = x_ref[...]
    h = h_ref[...]
    sup_ref[:, :w] = x
    sup_ref[:, w : 2 * w] = h
    values = sup_ref[:, : 2 * w]
    first = nn(sel, values)

    for fetch in fetches[2:4]:
        fetch.wait()
    for side, (tiles, cols) in enumerate(((ft_ref, fc_ref), (rt_ref, rc_ref))):
        for i in range(rows_i):
            for b in range(blocks):
                acc = None
                for t in range(tpr):
                    keep = (cols[i, t] == b).astype(F32)
                    term = tiles[i, t].astype(F32) * keep
                    acc = term if acc is None else acc + term
                r0 = side * nodes + i * tile
                a_ref[r0 : r0 + tile, b * tile : (b + 1) * tile] = acc.astype(BF16)
                at_ref[b * tile : (b + 1) * tile, r0 : r0 + tile] = acc.T.astype(BF16)

    pl.semaphore_wait(barrier, n - 1)
    rims[0].start(first)

    own = a_ref[:, :nodes]
    af_sent = nn(sel, a_ref[:nodes, :]).astype(BF16)
    ar_sent = nn(sel, a_ref[nodes:, :]).astype(BF16)
    sent13 = [nn(m[:, :nodes], values) for m in (af_sent, ar_sent)]
    local13 = nn(own, values)

    for fetch in fetches[4:]:
        fetch.wait()

    def widen(weight, columns, outs):
        pieces = []
        for k in range(KS):
            low = weight[k * CH : k * CH + half]
            high = weight[k * CH + half : (k + 1) * CH]
            pieces += [low, low, high, high]
        tall = jnp.concatenate(pieces, 0)
        i = lax.broadcasted_iota(jnp.int32, (columns, outs), 0)
        j = lax.broadcasted_iota(jnp.int32, (columns, outs), 1)
        pick = jnp.where(i == (j // w) * half + j % half, 1.0, 0.0).astype(BF16)
        wide = nn(tall, pick)
        i = lax.broadcasted_iota(jnp.int32, wide.shape, 0)
        j = lax.broadcasted_iota(jnp.int32, wide.shape, 1)
        return jnp.where((i // half) % 2 == (j // half) % 2, wide, 0.0).astype(BF16)

    wgx[...] = widen(wg_ref[...], 2 * HID, 2 * w)
    wcx[...] = widen(wc_ref[...].astype(F32).T.astype(BF16), HID, w)
    atf, atr = at_ref[:, :nodes], at_ref[:, nodes:]
    af_back = nn(atf[nodes:], sel_t).astype(BF16)
    ar_back = nn(atr[nodes:], sel_t).astype(BF16)

    gate_bias = jnp.broadcast_to(gate_bias_ref[...], (8, w))
    turned = pltpu.roll(gate_bias, half, 1)
    low8 = lax.broadcasted_iota(jnp.int32, (8, w), 1) < half
    reset_bias = jnp.where(low8, gate_bias, turned)[:1]
    update_bias = jnp.where(low8, turned, gate_bias)[:1]
    cand_bias = jnp.concatenate([cand_bias_ref[...]] * 2, 1)

    rim = rims[0].arrived()
    sent = [m + nn(a[:, nodes:], rim) for m, a in zip(sent13, (af_sent, ar_sent))]
    rims[1].start(jnp.concatenate(sent, 1))
    s13 = local13 + nn(a_ref[:, nodes:], rim)
    s1 = s13[:nodes].astype(BF16)
    s3 = s13[nodes:].astype(BF16)
    sup_ref[:, 2 * w : 4 * w] = s1
    sup_ref[:, 6 * w : 8 * w] = s3
    base = values.astype(F32)
    l2 = nn(a_ref[:nodes, :nodes], s1)
    l4 = nn(a_ref[nodes:, :nodes], s3)
    pre = nn(values, wgx[: 2 * w]) + nn(s1, wgx[2 * w : 4 * w]) + nn(s3, wgx[6 * w : 8 * w])
    rim = rims[1].arrived()
    l2 += nn(a_ref[:nodes, nodes:], rim[:, : 2 * w])
    l4 += nn(a_ref[nodes:, nodes:], rim[:, 2 * w :])
    s2 = (2.0 * l2 - base).astype(BF16)
    s4 = (2.0 * l4 - base).astype(BF16)
    sup_ref[:, 4 * w : 6 * w] = s2
    sup_ref[:, 8 * w :] = s4
    pre += nn(s2, wgx[4 * w : 6 * w]) + nn(s4, wgx[8 * w :])
    hf = h.astype(F32)
    reset = jax.nn.sigmoid(pre[:, :w] + reset_bias)
    update = jax.nn.sigmoid(pre[:, w:] + update_bias)

    gated = (reset * hf).astype(BF16)
    rims[2].start(nn(sel, gated))
    cand_ref[:, :w] = gated
    sent13 = [nn(m[:, :nodes], gated) for m in (af_sent, ar_sent)]
    l13 = nn(own, gated)
    cpre = nn(gated, wcx[w : 2 * w])
    for k in range(KS):
        cpre += nn(sup_ref[:, 2 * k * w : (2 * k + 1) * w], wcx[2 * k * w : (2 * k + 1) * w])
    rim = rims[2].arrived()
    sent = [m + nn(a[:, nodes:], rim) for m, a in zip(sent13, (af_sent, ar_sent))]
    rims[3].start(jnp.concatenate(sent, 1))
    l13 += nn(a_ref[:, nodes:], rim)
    t1 = l13[:nodes].astype(BF16)
    t3 = l13[nodes:].astype(BF16)
    cand_ref[:, w : 2 * w] = t1
    cand_ref[:, 3 * w : 4 * w] = t3
    l2 = nn(a_ref[:nodes, :nodes], t1)
    l4 = nn(a_ref[nodes:, :nodes], t3)
    cpre += nn(t1, wcx[3 * w : 4 * w]) + nn(t3, wcx[7 * w : 8 * w])
    rim = rims[3].arrived()
    l2 += nn(a_ref[:nodes, nodes:], rim[:, :w])
    l4 += nn(a_ref[nodes:, nodes:], rim[:, w:])
    gatedf = gated.astype(F32)
    t2 = (2.0 * l2 - gatedf).astype(BF16)
    t4 = (2.0 * l4 - gatedf).astype(BF16)
    cand_ref[:, 2 * w : 3 * w] = t2
    cand_ref[:, 4 * w :] = t4
    cpre += nn(t2, wcx[5 * w : 6 * w]) + nn(t4, wcx[9 * w :])
    cand = jnp.tanh(cpre + cand_bias)

    cot = cot_ref[...].astype(F32)
    update_grad = cot * (hf - cand)
    cg = (cot * (1.0 - update) * (1.0 - cand * cand)).astype(BF16)
    gu = (update_grad * update * (1.0 - update)).astype(BF16)

    def cand_cot(k, part):
        r0 = (2 * k + part) * w
        return nt(cg, wcx[r0 : r0 + w])

    c2, c4 = cand_cot(2, 1), cand_cot(4, 1)
    c2b, c4b = c2.astype(BF16), c4.astype(BF16)
    rims[4].start(jnp.concatenate([nn(atf[nodes:], c2b), nn(atr[nodes:], c4b)], 1))
    f1 = cand_cot(1, 1) + 2.0 * nn(atf[:nodes], c2b)
    f3 = cand_cot(3, 1) + 2.0 * nn(atr[:nodes], c4b)
    rest_h = cand_cot(0, 1) - c2 - c4
    f1b, f3b = f1.astype(BF16), f3.astype(BF16)
    sent = nn(atf[nodes:], f1b) + nn(atr[nodes:], f3b)
    rest_h += nn(atf[:nodes], f1b) + nn(atr[:nodes], f3b)

    low = lax.broadcasted_iota(jnp.int32, (half, w), 1) < half

    def fold(m):
        t = jnp.where(low[:1] if m[0].shape[0] == 1 else low, m[0], m[1])
        return t + pltpu.roll(t, half, 1)

    def colsum(v):
        s = jnp.sum(v.astype(F32), 0, keepdims=True)
        s = jnp.broadcast_to(s, (8, w))
        return s + pltpu.roll(s, half, 1)

    def both(mx, mh):
        return [fold((mx[:half], mx[half:])), fold((mh[:half], mh[half:]))]

    for k in range(KS):
        sx = sup_ref[:, 2 * k * w : (2 * k + 1) * w]
        sh = sup_ref[:, (2 * k + 1) * w : (2 * k + 2) * w]
        th = cand_ref[:, k * w : (k + 1) * w]
        yc = both(tn(sx, cg), tn(th, cg))
        yu = both(tn(sx, gu), tn(sh, gu))
        for part in range(2):
            r0 = k * CH + part * half
            sum1.stage[r0 : r0 + half] = jnp.where(low, yc[part], yu[part])
    used = KS * CH
    sum1.stage[used : used + 8] = jnp.where(low8, colsum(cg), colsum(gu))
    if sum1.stage.shape[0] > used + 8:
        sum1.stage[used + 8 :] = jnp.zeros((sum1.stage.shape[0] - used - 8, w), F32)
    sum1.phase1()

    rim = rims[4].arrived()
    sent += 2.0 * (nn(af_back, rim[:, :w]) + nn(ar_back, rim[:, w:]))
    rims[5].start(sent)
    back = (2.0 * nn(sel_t, rim)).astype(BF16)
    rest_h += nn(atf[:nodes], back[:, :w]) + nn(atr[:nodes], back[:, w:])
    for k in range(KS):
        rows = slice(2 * k * w, 2 * (k + 1) * w)
        part = nt(gu, wgx[rows, w:])
        g_ref[:, 2 * k * w : (2 * k + 1) * w] = part[:, :w] + cand_cot(k, 0)
        g_ref[:, (2 * k + 1) * w : 2 * (k + 1) * w] = part[:, w:]
    gated_grad = rest_h + nn(sel_t, rims[5].arrived())

    gr = (gated_grad * hf * reset * (1.0 - reset)).astype(BF16)

    def gate_cot(k):
        cols = slice(2 * k * w, 2 * (k + 1) * w)
        return g_ref[:, cols] + nt(gr, wgx[cols, :w])

    g2, g4 = gate_cot(2), gate_cot(4)
    g2b, g4b = g2.astype(BF16), g4.astype(BF16)
    rims[6].start(jnp.concatenate([nn(atf[nodes:], g2b), nn(atr[nodes:], g4b)], 1))
    f1 = gate_cot(1) + 2.0 * nn(atf[:nodes], g2b)
    f3 = gate_cot(3) + 2.0 * nn(atr[:nodes], g4b)
    rest_all = gate_cot(0) - g2 - g4
    f1b, f3b = f1.astype(BF16), f3.astype(BF16)
    sent = nn(atf[nodes:], f1b) + nn(atr[nodes:], f3b)
    folded = []
    for k in range(KS):
        sx = sup_ref[:, 2 * k * w : (2 * k + 1) * w]
        sh = sup_ref[:, (2 * k + 1) * w : (2 * k + 2) * w]
        folded += both(tn(sx, gr), tn(sh, gr))
    for m in range(KS):
        sum2.stage[m * half : (m + 1) * half] = jnp.where(low, folded[m], folded[m + KS])
    used = KS * half
    sum2.stage[used : used + 8] = colsum(gr)
    if sum2.stage.shape[0] > used + 8:
        sum2.stage[used + 8 :] = jnp.zeros((sum2.stage.shape[0] - used - 8, w), F32)
    sum2.phase1()
    sum1.phase2()

    rim = rims[6].arrived()
    sent += 2.0 * (nn(af_back, rim[:, : 2 * w]) + nn(ar_back, rim[:, 2 * w :]))
    rims[7].start(sent)
    back = (2.0 * nn(sel_t, rim)).astype(BF16)
    rest_all += nn(atf[:nodes], f1b) + nn(atr[:nodes], f3b)
    rest_all += nn(atf[:nodes], back[:, : 2 * w]) + nn(atr[:nodes], back[:, 2 * w :])
    sum2.phase2()
    sum1.phase3()
    used = KS * CH
    total1 = sum1.out[...].reshape(-1, w)[: used + 8].astype(F32) * scale
    cand_grad_ref[...] = total1[:used].T[:half]
    cand_bias_grad_ref[...] = total1[used : used + 1, :half]
    rest_all += nn(sel_t, rims[7].arrived())
    in_grad_ref[...] = rest_all[:, :w]
    state_grad_ref[...] = cot * update + gated_grad * reset + rest_all[:, w:]
    sum2.phase3()
    used2 = used // 2
    total2 = sum2.out[...].reshape(-1, w)[: used2 + 8].astype(F32) * scale
    gate_bias_grad_ref[...] = jnp.where(low8, total2[used2:], total1[used:])[:1]
    wide = jnp.broadcast_to(low[:1], (used2, w))
    gate_grad_ref[:used2] = jnp.where(wide, total2[:used2], total1[:used2])
    gate_grad_ref[used2:] = jnp.where(wide, pltpu.roll(total2[:used2], half, 1), total1[used2:used])
    for rim in rims:
        rim.finish()
    sum1.finish()
    sum2.finish()


def deliver_kernel(count, *refs):
    sources, targets, held = refs[:count], refs[count : 2 * count], refs[2 * count : 3 * count]
    in_sem, out_sem = refs[3 * count :]
    loads = [
        pltpu.make_async_copy(sources[i], held[i], in_sem.at[i]) for i in range(count)
    ]
    stores = [
        pltpu.make_async_copy(held[i], targets[i], out_sem.at[i]) for i in range(count)
    ]
    for load in loads:
        load.start()
    for load, store in zip(loads, stores):
        load.wait()
        store.start()
    for store in stores:
        store.wait()


def deliver(arrays):
    count = len(arrays)
    shapes = [(a.shape, a.dtype) for a in arrays]
    hbm = pl.BlockSpec(memory_space=pltpu.HBM)
    return pl.pallas_call(
        functools.partial(deliver_kernel, count),
        name="deliver",
        out_shape=tuple(jax.ShapeDtypeStruct(*shape) for shape in shapes),
        in_specs=[hbm] * count,
        out_specs=(hbm,) * count,
        scratch_shapes=[pltpu.VMEM(*shape) for shape in shapes]
        + [pltpu.SemaphoreType.DMA((count,))] * 2,
        compiler_params=pltpu.CompilerParams(vmem_limit_bytes=60 * 1024 * 1024),
    )(*arrays)


def on_device(
    layer_input,
    hidden_state,
    hidden_grad,
    gate_weight,
    gate_bias,
    candidate_weight,
    candidate_bias,
    forward_tiles,
    forward_columns,
    reverse_tiles,
    reverse_columns,
    send_rows,
    send_count,
):
    ng, nb = lax.axis_size("graph"), lax.axis_size("batch")
    nodes, w = layer_input.shape
    set_count, slot = send_rows.shape[1:]
    halo = set_count * slot
    r1 = chunk_rows(KS * CH + 8, ng * nb)
    r2 = chunk_rows(KS * CH // 2 + 8, ng * nb)
    widths = (2 * w, 4 * w, w, 2 * w, 2 * w, w, 4 * w, 2 * w)
    scratch = [
        pltpu.VMEM((KS * 2 * w, 2 * w), BF16),
        pltpu.VMEM((KS * 2 * w, w), BF16),
        pltpu.VMEM((2 * nodes, nodes + halo), BF16),
        pltpu.VMEM((nodes + halo, 2 * nodes), BF16),
        pltpu.VMEM((nodes, KS * 2 * w), BF16),
        pltpu.VMEM((nodes, KS * w), BF16),
        pltpu.VMEM((nodes, KS * 2 * w), F32),
    ]
    dma = lambda count: pltpu.SemaphoreType.DMA((count,))
    for width in widths:
        scratch += [
            pltpu.VMEM((halo, width), BF16),
            pltpu.VMEM((halo, width), BF16),
            dma(set_count),
            dma(set_count),
        ]
    n = nb * ng
    for r in (r1, r2):
        scratch += [
            pltpu.VMEM((n * r, w), F32),
            pltpu.VMEM((n, r, w), BF16),
            pltpu.VMEM((n, r, w), BF16),
            pltpu.VMEM((n, r, w), BF16),
        ]
        scratch += [dma(n)] * 4
    fetched = (
        layer_input,
        hidden_state,
        forward_tiles,
        reverse_tiles,
        gate_weight,
        candidate_weight.T,
        gate_bias.reshape(1, 2 * HID),
        candidate_bias.reshape(1, HID),
        hidden_grad,
    )
    scratch += [pltpu.VMEM(a.shape, a.dtype) for a in fetched] + [dma(len(fetched))]
    vmem = pl.BlockSpec(memory_space=pltpu.VMEM)
    hbm = pl.BlockSpec(memory_space=pltpu.HBM)
    smem = pl.BlockSpec(memory_space=pltpu.SMEM)
    scale = 1.0 / math.sqrt(nodes * ng * (w // HID) * nb)
    grads = pl.pallas_call(
        functools.partial(step_kernel, ng, nb, scale),
        name="gru_backward",
        out_shape=(
            jax.ShapeDtypeStruct((nodes, w), F32),
            jax.ShapeDtypeStruct((nodes, w), F32),
            jax.ShapeDtypeStruct((KS * CH, 2 * HID), F32),
            jax.ShapeDtypeStruct((1, 2 * HID), F32),
            jax.ShapeDtypeStruct((HID, KS * CH), F32),
            jax.ShapeDtypeStruct((1, HID), F32),
        ),
        in_specs=[hbm] * 8 + [smem, hbm, smem, vmem, smem],
        out_specs=(vmem,) * 6,
        scratch_shapes=scratch,
        compiler_params=pltpu.CompilerParams(
            collective_id=0, has_side_effects=True, vmem_limit_bytes=60 * 1024 * 1024
        ),
    )(
        layer_input,
        hidden_state,
        hidden_grad,
        gate_weight,
        gate_bias.reshape(1, 2 * HID),
        candidate_weight.T,
        candidate_bias.reshape(1, HID),
        forward_tiles,
        forward_columns,
        reverse_tiles,
        reverse_columns,
        send_rows,
        send_count,
    )
    input_grad, state_grad, gate_grad, gate_bias_grad, cand_grad, cand_bias_grad = deliver(grads)
    return (
        input_grad,
        state_grad,
        gate_grad,
        gate_bias_grad.reshape(2 * HID),
        cand_grad.T,
        cand_bias_grad.reshape(HID),
    )


def solution(mesh):
    placed = (
        P("graph", "batch"),
        P("graph", "batch"),
        P("graph", "batch"),
        P(),
        P(),
        P(),
        P(),
        P("graph", None, None, None),
        P("graph", None),
        P("graph", None, None, None),
        P("graph", None),
        P("graph", None, None),
        P("graph", None),
    )
    return jax.shard_map(
        on_device,
        mesh=mesh,
        in_specs=placed,
        out_specs=(P("graph", "batch"), P("graph", "batch"), P(), P(), P(), P()),
        check_vma=False,
    )
```
